1024 devices in a mesh: bx: 64 (over y, z_lo, core), by: 16 (over z_hi, x).
Axes of the slice: x: 4, y: 8, z: 16 (z_hi: 4, z_lo: 4; z = z_hi * 4 + z_lo), core: 2. Of those that a mesh axis runs over, the one named last changes fastest.
Arguments:
- populations: float32 [64, 16, 2, 19, 16, 256], P('bx', 'by'), may hold values from 0.019 to 0.467, as said below
- live_blocks: int32 [64, 16, 2], replicated, may hold values from 0 to 1, as said below
- moving: int32 [64, 16, 2], replicated, may hold values from 0 to 1, as said below
Outputs:
- final_populations: float32 [64, 16, 2, 19, 16, 256], P('bx', 'by')
The draws below stay inside these ranges and needn't reach their ends.
Inputs may be any that keep to these rules, and one draw needn't show every extreme that they name: `populations`: each entry is a positive population between 0.7 and 1.4 times its lattice weight w_q. `live_blocks`: 1 marks a fluid block and 0 a solid one. `moving`: the devices with bx indices 2p and 2p + 1 and the same by index form a pair; 1 stands only on fluid blocks of the device of a pair that has more fluid blocks, and that device marks exactly half the difference of the two devices' fluid counts, rounded down.
All inputs are finite; a program needn't handle non-finite values.
Results may differ from the reference program's by a relative error of at most 0.0001.
Values sent between devices are 32-bit elements; how exact they have to be, the bound alone decides.
A program may use at most 32 MiB of HBM per device.

```python
import jax
import jax.numpy as jnp
from jax import lax

BS = 16
BZ = 2
STEPS = 2
NX = 1024
NY = 256
NZ = 32
N_BX = 64
N_BY = 16


def draw_populations(key, part):
    weights = jnp.array([1.0 / 3.0] + [1.0 / 18.0] * 6 + [1.0 / 36.0] * 12, jnp.float32).reshape(1, 1, 1, 19, 1, 1)
    shape = (N_BX, N_BY, BZ, 19, BS, BS * BS)
    log_draw = jax.random.uniform(key, shape, jnp.float32, jnp.log(0.7), jnp.log(1.4))
    factor = jnp.exp(log_draw)
    return (weights * factor).astype(jnp.float32)


def block_tables(key):
    base_key = jax.random.fold_in(key, 11)
    pick_key, roll_key, score_key = jax.random.split(base_key, 3)
    heavy_side = jax.random.randint(pick_key, (N_BX // 2, 1, N_BY, 1), 0, 2)
    roll_draw = jax.random.randint(roll_key, (N_BX // 2, 2, N_BY, BZ), 0, 8)
    pair_sides = jnp.arange(2, dtype=jnp.int32).reshape(1, 2, 1, 1)
    limits = jnp.where(pair_sides == heavy_side, 7, 3)
    live_draw = (roll_draw < limits).astype(jnp.int32)
    counts = jnp.sum(live_draw, axis=3, keepdims=True).astype(jnp.int32)
    excess = (counts - counts[:, ::-1]) // 2
    scores = jax.random.randint(score_key, (N_BX // 2, 2, N_BY, BZ), 0, 1 << 20) * BZ
    scores = scores + jnp.arange(BZ, dtype=jnp.int32).reshape(1, 1, 1, BZ)
    scores = jnp.where(live_draw > 0, scores, -1)
    higher = jnp.sum((scores[..., None, :] > scores[..., :, None]).astype(jnp.int32), axis=-1).astype(jnp.int32)
    moving = ((live_draw > 0) & (higher < excess)).astype(jnp.int32)
    return (live_draw.reshape(N_BX, N_BY, BZ), moving.reshape(N_BX, N_BY, BZ))


def draw_live_blocks(key, part):
    return block_tables(key)[0]


def draw_moving(key, part):
    return block_tables(key)[1]


def setup_inputs(seed: int = 0) -> dict:
    streams_of = jax.random.split(jax.random.key(seed), 4)
    populations = draw_populations(jax.random.fold_in(streams_of[3], 71), 0)
    live_blocks = draw_live_blocks(jax.random.fold_in(streams_of[3], 71), 0)
    moving = draw_moving(jax.random.fold_in(streams_of[3], 71), 0)
    return dict(populations=populations, live_blocks=live_blocks, moving=moving)


VELOCITIES = [(0, 0, 0), (1, 0, 0), (-1, 0, 0), (0, 1, 0), (0, -1, 0), (0, 0, 1), (0, 0, -1), (1, 1, 0), (-1, -1, 0), (1, -1, 0), (-1, 1, 0), (1, 0, 1), (-1, 0, -1), (1, 0, -1), (-1, 0, 1), (0, 1, 1), (0, -1, -1), (0, 1, -1), (0, -1, 1)]
WEIGHTS = [1.0 / 3.0] + [1.0 / 18.0] * 6 + [1.0 / 36.0] * 12
OPPOSITE = [0, 2, 1, 4, 3, 6, 5, 8, 7, 10, 9, 12, 11, 14, 13, 16, 15, 18, 17]
TAU_BASE = 0.6
SMAG_COEF = 18.0 * 2.0 ** 0.5 * 0.17 ** 2

def column(values, dim_count):
    return jnp.array(values, jnp.float32).reshape((19,) + (1,) * (dim_count - 1))

def collide(distribution):
    dim_count = distribution.ndim
    comp_x = column([v[0] for v in VELOCITIES], dim_count)
    comp_y = column([v[1] for v in VELOCITIES], dim_count)
    comp_z = column([v[2] for v in VELOCITIES], dim_count)
    weight = column(WEIGHTS, dim_count)
    density = lax.optimization_barrier(jnp.sum(distribution, 0))
    vel_x = lax.optimization_barrier(jnp.sum(comp_x * distribution, 0)) / density
    vel_y = lax.optimization_barrier(jnp.sum(comp_y * distribution, 0)) / density
    vel_z = lax.optimization_barrier(jnp.sum(comp_z * distribution, 0)) / density
    project = comp_x * vel_x + comp_y * vel_y + comp_z * vel_z
    speed_sq = vel_x * vel_x + vel_y * vel_y + vel_z * vel_z
    equil = weight * density * (1.0 + 3.0 * project + 4.5 * project * project - 1.5 * speed_sq)
    noneq = distribution - equil
    stress_xx = lax.optimization_barrier(jnp.sum(comp_x * comp_x * noneq, 0))
    stress_yy = lax.optimization_barrier(jnp.sum(comp_y * comp_y * noneq, 0))
    stress_zz = lax.optimization_barrier(jnp.sum(comp_z * comp_z * noneq, 0))
    stress_xy = lax.optimization_barrier(jnp.sum(comp_x * comp_y * noneq, 0))
    stress_xz = lax.optimization_barrier(jnp.sum(comp_x * comp_z * noneq, 0))
    stress_yz = lax.optimization_barrier(jnp.sum(comp_y * comp_z * noneq, 0))
    strength = jnp.sqrt(stress_xx * stress_xx + stress_yy * stress_yy + stress_zz * stress_zz + 2.0 * (stress_xy * stress_xy + stress_xz * stress_xz + stress_yz * stress_yz))
    relax_time = 0.5 * (TAU_BASE + jnp.sqrt(TAU_BASE * TAU_BASE + SMAG_COEF * strength / density))
    return distribution - noneq / relax_time

def to_lattice(blocks):
    cube_view = blocks.reshape(N_BX, N_BY, BZ, 19, BS, BS, BS)
    cube_view = jnp.transpose(cube_view, (3, 0, 4, 1, 5, 2, 6))
    return cube_view.reshape(19, NX, NY, NZ)

def to_blocks(lattice):
    cube_view = lattice.reshape(19, N_BX, BS, N_BY, BS, BZ, BS)
    cube_view = jnp.transpose(cube_view, (1, 3, 5, 0, 2, 4, 6))
    return cube_view.reshape(N_BX, N_BY, BZ, 19, BS, BS * BS)

def reference(populations, live_blocks, moving):
    live_mask = live_blocks > 0
    slot_order = (jnp.cumsum(live_mask.astype(jnp.int32), axis=2) - 1).astype(jnp.int32)
    slot_order = jnp.clip(slot_order, 0, BZ - 1).astype(jnp.int32)
    picked = jnp.take_along_axis(populations, slot_order[:, :, :, None, None, None], axis=2)
    blocks = jnp.where(live_mask[:, :, :, None, None, None], picked, 0.0)
    lattice = to_lattice(blocks)
    fluid_cells = jnp.repeat(jnp.repeat(jnp.repeat(live_mask, BS, 0), BS, 1), BS, 2)
    fluid_slabs = fluid_cells.reshape(N_BX, BS, NY, NZ)
    weight_col = column(WEIGHTS, 4)

    def one_slab(items):
        distribution, alive_cells = items
        safe_dist = jnp.where(alive_cells, distribution, weight_col)
        return jnp.where(alive_cells, collide(safe_dist), 0.0)
    for turn_index in range(STEPS):
        slab_view = jnp.transpose(lattice.reshape(19, N_BX, BS, NY, NZ), (1, 0, 2, 3, 4))
        relaxed = lax.map(one_slab, (slab_view, fluid_slabs))
        relaxed = jnp.transpose(relaxed, (1, 0, 2, 3, 4)).reshape(19, NX, NY, NZ)
        moved_list = []
        for index in range(19):
            offset = VELOCITIES[index]
            arriving = jnp.roll(relaxed[index], offset, axis=(0, 1, 2))
            source = jnp.roll(fluid_cells, offset, axis=(0, 1, 2))
            bounced = jnp.where(fluid_cells, relaxed[OPPOSITE[index]], 0.0)
            moved_list.append(jnp.where(source & fluid_cells, arriving, bounced))
        lattice = jnp.stack(moved_list)
    final = to_blocks(lattice)
    kept_blocks = live_mask & (moving == 0)
    arrive = (moving > 0).reshape(N_BX // 2, 2, N_BY, BZ)[:, ::-1].reshape(N_BX, N_BY, BZ)
    usable = jnp.concatenate([kept_blocks, arrive], axis=2)
    list_rank = (jnp.cumsum(usable.astype(jnp.int32), axis=2) - 1).astype(jnp.int32)
    slot_ids = jnp.arange(BZ, dtype=jnp.int32)
    slot_hit = usable[:, :, None, :] & (list_rank[:, :, None, :] == slot_ids[None, None, :, None])
    positions = jnp.arange(2 * BZ, dtype=jnp.int32)
    source = lax.optimization_barrier(jnp.sum(jnp.where(slot_hit, positions, 0), axis=3)).astype(jnp.int32)
    present = jnp.any(slot_hit, axis=3)
    pair_blocks = final.reshape(N_BX // 2, 2, N_BY, BZ, 19, BS, BS * BS)
    pair_source = source.reshape(N_BX // 2, 2, N_BY, BZ)
    pair_present = present.reshape(N_BX // 2, 2, N_BY, BZ)

    def one_pair(items):
        pair_data, pair_picks, pair_mask = items
        results = []
        for member in range(2):
            candidates = jnp.concatenate([pair_data[member], pair_data[1 - member]], axis=1)
            chosen = jnp.take_along_axis(candidates, pair_picks[member][:, :, None, None, None], axis=1)
            results.append(jnp.where(pair_mask[member][:, :, None, None, None], chosen, 0.0))
        return jnp.stack(results)
    placed = lax.map(one_pair, (pair_blocks, pair_source, pair_present))
    return placed.reshape(N_BX, N_BY, BZ, 19, BS, BS * BS)
```

```python
import functools

import jax
import jax.numpy as jnp
from jax import lax
from jax.experimental import pallas as pl
from jax.experimental.pallas import tpu as pltpu
from jax.sharding import PartitionSpec as P

MESH = pl.DeviceIdType.MESH
VELOCITIES = [
    (0, 0, 0), (1, 0, 0), (-1, 0, 0), (0, 1, 0), (0, -1, 0), (0, 0, 1), (0, 0, -1),
    (1, 1, 0), (-1, -1, 0), (1, -1, 0), (-1, 1, 0), (1, 0, 1), (-1, 0, -1),
    (1, 0, -1), (-1, 0, 1), (0, 1, 1), (0, -1, -1), (0, 1, -1), (0, -1, 1),
]
OPPOSITE = [0, 2, 1, 4, 3, 6, 5, 8, 7, 10, 9, 12, 11, 14, 13, 16, 15, 18, 17]
SMAG_COEF = 18.0 * 2.0**0.5 * 0.17**2
SOLID = -1e30
SOLID_TEST = -1e29
RING_Y = ([3, 7, 10, 15, 17], [4, 8, 9, 16, 18])
F32 = jnp.float32


def collide(f):
    sums, diffs = {}, {}
    for i in range(1, 19, 2):
        sums[i] = f[i] + f[i + 1]
        diffs[i] = f[i] - f[i + 1]
    side_xy = sums[7] + sums[9]
    side_xz = sums[11] + sums[13]
    side_yz = sums[15] + sums[17]
    density = f[0] + (sums[1] + sums[3] + sums[5]) + (side_xy + side_xz + side_yz)
    mom_x = diffs[1] + (diffs[7] + diffs[9]) + (diffs[11] + diffs[13])
    mom_y = diffs[3] + (diffs[7] - diffs[9]) + (diffs[15] + diffs[17])
    mom_z = diffs[5] + (diffs[11] - diffs[13]) + (diffs[15] - diffs[17])
    inverse = 1.0 / density
    vel_x, vel_y, vel_z = mom_x * inverse, mom_y * inverse, mom_z * inverse
    third = density * (1.0 / 3.0)
    p_xx = sums[1] + side_xy + side_xz - third - mom_x * vel_x
    p_yy = sums[3] + side_xy + side_yz - third - mom_y * vel_y
    p_zz = sums[5] + side_xz + side_yz - third - mom_z * vel_z
    p_xy = sums[7] - sums[9] - mom_x * vel_y
    p_xz = sums[11] - sums[13] - mom_x * vel_z
    p_yz = sums[15] - sums[17] - mom_y * vel_z
    strength = jnp.sqrt(
        p_xx * p_xx + p_yy * p_yy + p_zz * p_zz + 2.0 * (p_xy * p_xy + p_xz * p_xz + p_yz * p_yz)
    )
    omega = 2.0 / (0.6 + jnp.sqrt(0.36 + SMAG_COEF * strength * inverse))
    keep = 1.0 - omega
    gain = omega * density
    speed = vel_x * vel_x + vel_y * vel_y + vel_z * vel_z
    base = 1.0 - 1.5 * speed
    edge, corner = gain * (1.0 / 18.0), gain * (1.0 / 36.0)
    base_edge, base_corner = edge * base, corner * base
    result = [None] * 19
    result[0] = f[0] * keep + (gain * (1.0 / 3.0)) * base
    along = {
        1: vel_x, 3: vel_y, 5: vel_z,
        7: vel_x + vel_y, 9: vel_x - vel_y, 11: vel_x + vel_z,
        13: vel_x - vel_z, 15: vel_y + vel_z, 17: vel_y - vel_z,
    }
    for i in range(1, 19, 2):
        weight, rest = (edge, base_edge) if i < 7 else (corner, base_corner)
        odd = 3.0 * weight * along[i]
        even = rest + (1.5 * odd) * along[i]
        result[i] = f[i] * keep + (even + odd)
        result[i + 1] = f[i + 1] * keep + (even - odd)
    return result


def lanes_of(shape):
    return lax.broadcasted_iota(jnp.int32, shape, len(shape) - 1)


def exchange(
    n_x, n_y, pop, live, move, col, xg, yg, cp, tab, fbuf, xs, ys, cs, in_sem, send_sem, recv_sem
):
    me_x, me_y = lax.axis_index("bx"), lax.axis_index("by")
    side = lax.rem(me_x, 2)
    mate = me_x + 1 - 2 * side
    outer = lax.rem(me_x + n_x - 1 + 2 * side, n_x)
    above = lax.rem(me_y + 1, n_y)
    below = lax.rem(me_y + n_y - 1, n_y)
    at_mate, at_outer = (mate, me_y), (outer, me_y)
    at_y = ((me_x, above), (me_x, below))

    barrier = pltpu.get_barrier_semaphore()
    for device in (at_mate, at_outer) + at_y:
        pl.semaphore_signal(barrier, inc=1, device_id=device, device_id_type=MESH)

    load_pop = pltpu.make_async_copy(pop, fbuf, in_sem.at[0])
    load_live = pltpu.make_async_copy(live.at[me_y], tab.at[0], in_sem.at[1])
    load_move = pltpu.make_async_copy(move.at[me_y], tab.at[1], in_sem.at[2])
    load_live.start()
    load_move.start()
    load_pop.start()
    load_live.wait()
    load_move.wait()
    load_pop.wait()

    row = tab[0]
    flags = jnp.sum(jnp.where(lanes_of(row.shape) == me_x, row, 0).astype(F32), axis=1, keepdims=True)
    first = jnp.broadcast_to(flags[0:1, :], (8, 128)) > 0.5
    second = jnp.broadcast_to(flags[1:2, :], (8, 128)) > 0.5

    for k in range(2):
        fluid = (first, second)[k]

        def relax(i, carry, k=k, fluid=fluid):
            tile, half = i // 2, i % 2
            rows = pl.ds(pl.multiple_of(half * 8, 8), 8)
            lanes = pl.ds(pl.multiple_of(tile * 128, 128), 128)
            f = [jnp.where(first, fbuf[k, q, rows, lanes], fbuf[1 - k, q, rows, lanes]) for q in range(19)]
            for q, value in enumerate(collide(f)):
                to = pl.ds(pl.multiple_of(q * 16 + half * 8, 8), 8)
                col[side, k, tile, to, :] = jnp.where(fluid, value, SOLID)
            return carry

        lax.fori_loop(0, 4, relax, 0)

    near, far = 15 * side, 1 + 13 * side
    for tile in range(2):
        for k in range(2):
            own = col.at[side, k, tile]
            xs[tile, k, 0:19, :] = own[pl.ds(near, 19, stride=16), :]
            xs[tile, k, 19:20, :] = own[pl.ds((2 - side) * 16 + far, 1), :]
            xs[tile, k, 20:24, :] = own[pl.ds((8 - side) * 16 + far, 4, stride=32), :]

    group = lanes_of((16, 128)) // 16

    def pack(k, carry):
        for way in range(2):
            tile, first_lane, second_lane = ((1, 112, 96), (0, 0, 16))[way]
            for g in range(3):
                packed = None
                for i in range(8):
                    p = 8 * g + i
                    q, lane = (p, first_lane) if p < 19 else (RING_Y[way][p - 19], second_lane)
                    value = col[side, k, tile, q * 16 : q * 16 + 16, :]
                    shift = (16 * i - lane) % 128
                    if shift:
                        value = pltpu.roll(value, shift, 1)
                    packed = value if packed is None else jnp.where(group == i, value, packed)
                ys[way, k, g] = packed
        return carry

    lax.fori_loop(0, 2, pack, 0)

    pl.semaphore_wait(barrier, 4)

    def send(index, source, target, device):
        copy = pltpu.make_async_remote_copy(
            src_ref=source,
            dst_ref=target,
            send_sem=send_sem.at[index],
            recv_sem=recv_sem.at[index],
            device_id=device,
            device_id_type=MESH,
        )
        copy.start()
        return copy

    to_outer = send(0, xs, xg.at[1 - side], at_outer)
    to_y = [send(1 + way, ys.at[way], yg.at[side, way], at_y[way]) for way in range(2)]
    whole = send(3, col.at[side], col.at[side], at_mate)

    to_outer.wait_recv()
    quarter = lanes_of((8, 128)) // 32
    for way in range(2):
        for k in range(2):
            packed = None
            for g in range(3):
                value = xg[side, 1 - way, k, 8 * g : 8 * g + 8, :]
                shift = (32 * g - (96, 0)[way]) % 128
                if shift:
                    value = pltpu.roll(value, shift, 1)
                packed = value if packed is None else jnp.where(quarter == g, value, packed)
            cs[way, k] = packed
    corners = [send(4 + way, cs.at[way], cp.at[side, way], at_y[way]) for way in range(2)]
    relays = [send(6, xg.at[side], xg.at[side], at_mate)]
    for way in range(2):
        to_y[way].wait_recv()
        relays.append(send(7 + way, yg.at[side, way], yg.at[side, way], at_mate))
    for way in range(2):
        corners[way].wait_recv()
        relays.append(send(9 + way, cp.at[side, way], cp.at[side, way], at_mate))
    whole.wait_recv()
    for copy in relays:
        copy.wait_recv()
    for copy in [to_outer, whole] + to_y + corners + relays:
        copy.wait_send()


def stream(source, q, row, tiles):
    _, step_y, step_z = VELOCITIES[q]
    need = sorted({(t - d) % 3 for t in tiles for d in ((0, step_y) if step_y else (0,))})
    data = [{t: source[k, t, pl.ds(row, 8), :] for t in need} for k in range(2)]
    lane = lanes_of((8, 128))

    def turn(value, shift):
        return pltpu.roll(value, shift % 128, 1) if shift % 128 else value

    if step_z:
        at_edge = lane % 16 == (0 if step_z == 1 else 15)
        moved = [
            {
                t: jnp.where(
                    at_edge,
                    turn(data[1 - k][t], 16 * step_y - 15 * step_z),
                    turn(data[k][t], 16 * step_y + step_z),
                )
                for t in need
            }
            for k in range(2)
        ]
    else:
        moved = [{t: turn(data[k][t], 16 * step_y) for t in need} for k in range(2)]
    if step_y:
        crossed = lane < 16 if step_y == 1 else lane >= 112
        moved = [
            {t: jnp.where(crossed, moved[k][(t - step_y) % 3], moved[k][t]) for t in tiles}
            for k in range(2)
        ]
    return moved


def advance(col, xg, yg, cp, tab, out, ext, nxt, ux, fs):
    me_x = lax.axis_index("bx")
    side = lax.rem(me_x, 2)
    mate = me_x + 1 - 2 * side

    def bit(table, device, k):
        row = tab[table]
        hit = (lanes_of(row.shape) == device) & (lax.broadcasted_iota(jnp.int32, row.shape, 0) == k)
        return jnp.sum(jnp.where(hit, row, 0).astype(F32))

    own_live = [bit(0, me_x, k) for k in range(2)]
    own_moving = [bit(1, me_x, k) for k in range(2)]
    arriving = [bit(1, mate, k) for k in range(2)]
    swap = (own_live[0] + own_live[1] < 0.5) & (arriving[0] + arriving[1] > 0.5)
    chosen = [
        jnp.where(swap, arriving[k], own_live[k] * (1.0 - own_moving[k])) > 0.5 for k in range(2)
    ]
    sc = jnp.where(swap, 1 - side, side)

    outer_near, outer_far = 7 + 17 * sc, 6 + 19 * sc
    inner_near, inner_far = 24 - 17 * sc, 25 - 19 * sc
    mate_near, mate_far = 15 * sc, 1 + 13 * sc
    lane8 = lanes_of((8, 128))

    def place_outer(k, tile, planes):
        ext[k, tile, pl.ds(outer_near, 19, stride=32), :] = planes[0:19, :]
        ext[k, tile, pl.ds((1 + sc) * 32 + outer_far, 1), :] = planes[19:20, :]
        ext[k, tile, pl.ds((7 + sc) * 32 + outer_far, 4, stride=64), :] = planes[20:24, :]

    for k in range(2):
        for tile in range(2):
            for q in range(19):
                ext[k, tile, q * 32 + 8 : q * 32 + 24, :] = col[sc, k, tile, q * 16 : q * 16 + 16, :]
            place_outer(k, tile, xg.at[sc, tile, k])
            ext[k, tile, pl.ds(inner_near, 19, stride=32), :] = col[
                1 - sc, k, tile, pl.ds(mate_near, 19, stride=16), :
            ]
            ext[k, tile, pl.ds(inner_far, 19, stride=32), :] = col[
                1 - sc, k, tile, pl.ds(mate_far, 19, stride=16), :
            ]
        for g in range(3):
            low = cp[sc, 0, k]
            high = cp[sc, 1, k]
            low = pltpu.roll(low, (96 - 32 * g) % 128, 1)
            high = pltpu.roll(high, (-32 * g) % 128, 1) if g else high
            ux[k, 8 * g : 8 * g + 8, :] = jnp.where(lane8 < 64, high, low)
        place_outer(k, 2, ux.at[k])

        for own in range(2):
            rows = 16 if own else 8
            lane = lanes_of((rows, 128))
            for q in range(19):
                parts = []
                for way in range(2):
                    near_lane, far_lane = ((112, 96), (0, 16))[way]

                    def unit(p, lane_to, way=way):
                        if own:
                            value = yg[sc, way, k, p // 8]
                        else:
                            value = yg[1 - sc, way, k, p // 8, pl.ds(pl.multiple_of(8 * sc, 8), 8), :]
                        shift = (lane_to - 16 * (p % 8)) % 128
                        return pltpu.roll(value, shift, 1) if shift else value

                    value = unit(q, near_lane)
                    if q in RING_Y[way]:
                        far = unit(19 + RING_Y[way].index(q), far_lane)
                        value = jnp.where(lane // 16 == near_lane // 16, value, far)
                    parts.append(value)
                value = jnp.where(lane < 64, parts[1], parts[0])
                if own:
                    ext[k, 2, q * 32 + 8 : q * 32 + 24, :] = value
                else:
                    ext[k, 2, pl.ds(pl.multiple_of(q * 32 + 24 - 24 * sc, 8), 8), :] = value

    def arrive(source, stride, base, q, row, tiles):
        moved = stream(source, q, q * stride + base + row - VELOCITIES[q][0], tiles)
        result = {}
        for k in range(2):
            for t in tiles:
                value = moved[k][t]
                if q:
                    back = source[k, t, pl.ds(OPPOSITE[q] * stride + base + row, 8), :]
                    value = jnp.where(value > SOLID_TEST, value, back)
                result[k, t] = value
        return result

    for chunk in range(3):
        for q in range(19):
            for (k, t), value in arrive(ext, 32, 7, q, 8 * chunk, (0, 1, 2)).items():
                fs[q, k, t] = value
        for k in range(2):
            for t in range(3):
                f = [fs[q, k, t] for q in range(19)]
                fluid = f[0] > SOLID_TEST
                for q, value in enumerate(collide(f)):
                    nxt[k, t, q * 24 + 8 * chunk : q * 24 + 8 * chunk + 8, :] = jnp.where(
                        fluid, value, SOLID
                    )

    zero = jnp.zeros((8, 128), F32)
    both = chosen[0] & chosen[1]
    for chunk in range(2):
        for q in range(19):
            values = arrive(nxt, 24, 1, q, 8 * chunk, (0, 1))
            for t in range(2):
                spot = (q, slice(8 * chunk, 8 * chunk + 8), slice(128 * t, 128 * t + 128))
                lower, upper = values[0, t], values[1, t]
                out[(0,) + spot] = jnp.where(chosen[0], lower, jnp.where(chosen[1], upper, zero))
                out[(1,) + spot] = jnp.where(both, upper, zero)


VMEM = pl.BlockSpec(memory_space=pltpu.VMEM)
HBM = pl.BlockSpec(memory_space=pltpu.HBM)


def shards(n_x, n_y, populations, live_blocks, moving):
    pop, live, move = (
        pltpu.with_memory_space_constraint(array, pltpu.HBM)
        for array in (
            populations.reshape(2, 19, 16, 256),
            jnp.transpose(live_blocks, (1, 2, 0)),
            jnp.transpose(moving, (1, 2, 0)),
        )
    )
    shapes = [(2, 2, 2, 304, 128), (2, 2, 2, 24, 128), (2, 2, 2, 3, 16, 128), (2, 2, 2, 8, 128)]
    parts = pl.pallas_call(
        functools.partial(exchange, n_x, n_y),
        out_shape=[jax.ShapeDtypeStruct(shape, F32) for shape in shapes]
        + [jax.ShapeDtypeStruct((2, 2, n_x), jnp.int32)],
        in_specs=[HBM] * 3,
        out_specs=[VMEM] * 5,
        scratch_shapes=[
            pltpu.VMEM((2, 19, 16, 256), F32),
            pltpu.VMEM((2, 2, 24, 128), F32),
            pltpu.VMEM((2, 2, 3, 16, 128), F32),
            pltpu.VMEM((2, 2, 8, 128), F32),
            pltpu.SemaphoreType.DMA((3,)),
            pltpu.SemaphoreType.DMA((11,)),
            pltpu.SemaphoreType.DMA((11,)),
        ],
        compiler_params=pltpu.CompilerParams(
            collective_id=0, has_side_effects=True, vmem_limit_bytes=8 << 20
        ),
        name="exchange",
    )(pop, live, move)
    result = pl.pallas_call(
        advance,
        out_shape=jax.ShapeDtypeStruct((2, 19, 16, 256), F32),
        in_specs=[VMEM] * 5,
        out_specs=VMEM,
        scratch_shapes=[
            pltpu.VMEM((2, 3, 19 * 32, 128), F32),
            pltpu.VMEM((2, 3, 19 * 24, 128), F32),
            pltpu.VMEM((2, 24, 128), F32),
            pltpu.VMEM((19, 2, 3, 8, 128), F32),
        ],
        compiler_params=pltpu.CompilerParams(vmem_limit_bytes=12 << 20),
        name="advance",
    )(*parts)
    return result.reshape(1, 1, 2, 19, 16, 256)


def solution(mesh):
    n_x, n_y = mesh.shape["bx"], mesh.shape["by"]
    placed = (P("bx", "by", None, None, None, None), P(), P())
    return jax.shard_map(
        functools.partial(shards, n_x, n_y),
        mesh=mesh,
        in_specs=placed,
        out_specs=P("bx", "by", None, None, None, None),
        check_vma=False,
    )
```

```python
import functools

import jax
import jax.numpy as jnp
from jax import lax
from jax.experimental import pallas as pl
from jax.experimental.pallas import tpu as pltpu
from jax.sharding import PartitionSpec as P

MESH = pl.DeviceIdType.MESH
VELOCITIES = [
    (0, 0, 0), (1, 0, 0), (-1, 0, 0), (0, 1, 0), (0, -1, 0), (0, 0, 1), (0, 0, -1),
    (1, 1, 0), (-1, -1, 0), (1, -1, 0), (-1, 1, 0), (1, 0, 1), (-1, 0, -1),
    (1, 0, -1), (-1, 0, 1), (0, 1, 1), (0, -1, -1), (0, 1, -1), (0, -1, 1),
]
OPPOSITE = [0, 2, 1, 4, 3, 6, 5, 8, 7, 10, 9, 12, 11, 14, 13, 16, 15, 18, 17]
SMAG_COEF = 18.0 * 2.0**0.5 * 0.17**2
SOLID = -1e30
SOLID_TEST = -1e29
RING_Y = ([3, 7, 10, 15, 17], [4, 8, 9, 16, 18])
F32 = jnp.float32


def collide(f):
    sums, diffs = {}, {}
    for i in range(1, 19, 2):
        sums[i] = f[i] + f[i + 1]
        diffs[i] = f[i] - f[i + 1]
    side_xy = sums[7] + sums[9]
    side_xz = sums[11] + sums[13]
    side_yz = sums[15] + sums[17]
    density = f[0] + (sums[1] + sums[3] + sums[5]) + (side_xy + side_xz + side_yz)
    mom_x = diffs[1] + (diffs[7] + diffs[9]) + (diffs[11] + diffs[13])
    mom_y = diffs[3] + (diffs[7] - diffs[9]) + (diffs[15] + diffs[17])
    mom_z = diffs[5] + (diffs[11] - diffs[13]) + (diffs[15] - diffs[17])
    inverse = 1.0 / density
    vel_x, vel_y, vel_z = mom_x * inverse, mom_y * inverse, mom_z * inverse
    third = density * (1.0 / 3.0)
    p_xx = sums[1] + side_xy + side_xz - third - mom_x * vel_x
    p_yy = sums[3] + side_xy + side_yz - third - mom_y * vel_y
    p_zz = sums[5] + side_xz + side_yz - third - mom_z * vel_z
    p_xy = sums[7] - sums[9] - mom_x * vel_y
    p_xz = sums[11] - sums[13] - mom_x * vel_z
    p_yz = sums[15] - sums[17] - mom_y * vel_z
    strength = jnp.sqrt(
        p_xx * p_xx + p_yy * p_yy + p_zz * p_zz + 2.0 * (p_xy * p_xy + p_xz * p_xz + p_yz * p_yz)
    )
    omega = 2.0 / (0.6 + jnp.sqrt(0.36 + SMAG_COEF * strength * inverse))
    keep = 1.0 - omega
    gain = omega * density
    speed = vel_x * vel_x + vel_y * vel_y + vel_z * vel_z
    base = 1.0 - 1.5 * speed
    edge, corner = gain * (1.0 / 18.0), gain * (1.0 / 36.0)
    base_edge, base_corner = edge * base, corner * base
    result = [None] * 19
    result[0] = f[0] * keep + (gain * (1.0 / 3.0)) * base
    along = {
        1: vel_x, 3: vel_y, 5: vel_z,
        7: vel_x + vel_y, 9: vel_x - vel_y, 11: vel_x + vel_z,
        13: vel_x - vel_z, 15: vel_y + vel_z, 17: vel_y - vel_z,
    }
    for i in range(1, 19, 2):
        weight, rest = (edge, base_edge) if i < 7 else (corner, base_corner)
        odd = 3.0 * weight * along[i]
        even = rest + (1.5 * odd) * along[i]
        result[i] = f[i] * keep + (even + odd)
        result[i + 1] = f[i + 1] * keep + (even - odd)
    return result


def lanes_of(shape):
    return lax.broadcasted_iota(jnp.int32, shape, len(shape) - 1)


def exchange(
    n_x, n_y, pop, live, move, col, xg, yg, cp, tab,
    fbuf, xs, ys, cs, in_sem, send_sem, recv_sem, ready,
):
    me_x, me_y = lax.axis_index("bx"), lax.axis_index("by")
    side = lax.rem(me_x, 2)
    base = me_x - side
    at_mate = (base + 1 - side, me_y)
    at_x = (
        (lax.rem(base + n_x - 1, n_x), me_y),
        (lax.rem(base + 3, n_x), me_y),
    )
    at_y = ((base + 1, lax.rem(me_y + 1, n_y)), (base + 1, lax.rem(me_y + n_y - 1, n_y)))
    barrier = pltpu.get_barrier_semaphore()

    @pl.when(side == 1)
    def _():
        for device in at_x + at_y + (at_mate,):
            pl.semaphore_signal(barrier, inc=1, device_id=device, device_id_type=MESH)

    load_pop = pltpu.make_async_copy(pop, fbuf.at[side], in_sem.at[0])
    load_live = pltpu.make_async_copy(live.at[me_y], tab.at[0], in_sem.at[1])
    load_move = pltpu.make_async_copy(move.at[me_y], tab.at[1], in_sem.at[2])
    load_pop.start()
    load_live.start()
    load_move.start()

    def link(index, source, target, device):
        return pltpu.make_async_remote_copy(
            src_ref=source,
            dst_ref=target,
            send_sem=send_sem.at[index],
            recv_sem=recv_sem.at[index],
            device_id=device,
            device_id_type=MESH,
        )

    raw = link(0, pop, fbuf.at[side], at_mate)

    @pl.when(side == 0)
    def _():
        pl.semaphore_wait(barrier, 1)
        pl.semaphore_signal(ready, inc=1, device_id=at_mate, device_id_type=MESH)
        raw.start()

    load_live.wait()
    load_move.wait()
    load_pop.wait()

    def relax_column(c):
        row = tab[0]
        hit = lanes_of(row.shape) == base + c
        flags = jnp.sum(jnp.where(hit, row, 0).astype(F32), axis=1, keepdims=True)
        first = jnp.broadcast_to(flags[0:1, :], (8, 128)) > 0.5
        second = jnp.broadcast_to(flags[1:2, :], (8, 128)) > 0.5
        for k in range(2):
            fluid = (first, second)[k]

            def relax(i, carry, k=k, fluid=fluid):
                tile, half = i // 2, i % 2
                rows = pl.ds(pl.multiple_of(half * 8, 8), 8)
                lanes = pl.ds(pl.multiple_of(tile * 128, 128), 128)
                f = [
                    jnp.where(first, fbuf[c, k, q, rows, lanes], fbuf[c, 1 - k, q, rows, lanes])
                    for q in range(19)
                ]
                for q, value in enumerate(collide(f)):
                    to = pl.ds(pl.multiple_of(q * 16 + half * 8, 8), 8)
                    col[c, k, tile, to, :] = jnp.where(fluid, value, SOLID)
                return carry

            lax.fori_loop(0, 4, relax, 0)

    group = lanes_of((16, 128)) // 16

    def pack_column(c):
        near, far = 15 * c, 1 + 13 * c
        for tile in range(2):
            for k in range(2):
                own = col.at[c, k, tile]
                xs[c, tile, k, 0:19, :] = own[pl.ds(near, 19, stride=16), :]
                xs[c, tile, k, 19:20, :] = own[pl.ds((2 - c) * 16 + far, 1), :]
                xs[c, tile, k, 20:24, :] = own[pl.ds((8 - c) * 16 + far, 4, stride=32), :]

        def pack(k, carry):
            for way in range(2):
                tile, first_lane, second_lane = ((1, 112, 96), (0, 0, 16))[way]
                for g in range(3):
                    packed = None
                    for i in range(8):
                        p = 8 * g + i
                        q, lane = (p, first_lane) if p < 19 else (RING_Y[way][p - 19], second_lane)
                        value = col[c, k, tile, q * 16 : q * 16 + 16, :]
                        shift = (16 * i - lane) % 128
                        if shift:
                            value = pltpu.roll(value, shift, 1)
                        packed = value if packed is None else jnp.where(group == i, value, packed)
                    ys[way, c, k, g] = packed
            return carry

        lax.fori_loop(0, 2, pack, 0)

    relax_column(side)

    @pl.when(side == 1)
    def _():
        pack_column(1)
        pl.semaphore_wait(ready, 1)
        raw.start()

    raw.wait_recv()
    relax_column(1 - side)

    relay = (
        [link(7, xg, xg, at_mate)]
        + [link(8 + way, yg.at[way], yg.at[way], at_mate) for way in range(2)]
        + [link(10, cp, cp, at_mate)]
    )

    @pl.when(side == 1)
    def _():
        pack_column(0)
        pl.semaphore_wait(barrier, 4)
        to_x = [link(1 + c, xs.at[c], xg.at[1 - c], at_x[c]) for c in range(2)]
        to_y = [link(3 + way, ys.at[way], yg.at[way], at_y[way]) for way in range(2)]
        for copy in to_x + to_y:
            copy.start()
        for copy in to_x:
            copy.wait_recv()
        quarter = lanes_of((8, 128)) // 32
        for way in range(2):
            for c in range(2):
                for k in range(2):
                    packed = None
                    for g in range(3):
                        value = xg[c, 1 - way, k, 8 * g : 8 * g + 8, :]
                        shift = (32 * g - (96, 0)[way]) % 128
                        if shift:
                            value = pltpu.roll(value, shift, 1)
                        packed = value if packed is None else jnp.where(quarter == g, value, packed)
                    cs[way, c, k] = packed
        corners = [link(5 + way, cs.at[way], cp.at[way], at_y[way]) for way in range(2)]
        for copy in corners:
            copy.start()
        relay[0].start()
        for way in range(2):
            to_y[way].wait_recv()
            relay[1 + way].start()
        for copy in corners:
            copy.wait_recv()
        relay[3].start()
        for copy in to_x + to_y + corners + relay:
            copy.wait_send()

    @pl.when(side == 0)
    def _():
        for copy in relay:
            copy.wait_recv()

    raw.wait_send()


def stream(source, q, row, tiles):
    _, step_y, step_z = VELOCITIES[q]
    need = sorted({(t - d) % 3 for t in tiles for d in ((0, step_y) if step_y else (0,))})
    data = [{t: source[k, t, pl.ds(row, 8), :] for t in need} for k in range(2)]
    lane = lanes_of((8, 128))

    def turn(value, shift):
        return pltpu.roll(value, shift % 128, 1) if shift % 128 else value

    if step_z:
        at_edge = lane % 16 == (0 if step_z == 1 else 15)
        moved = [
            {
                t: jnp.where(
                    at_edge,
                    turn(data[1 - k][t], 16 * step_y - 15 * step_z),
                    turn(data[k][t], 16 * step_y + step_z),
                )
                for t in need
            }
            for k in range(2)
        ]
    else:
        moved = [{t: turn(data[k][t], 16 * step_y) for t in need} for k in range(2)]
    if step_y:
        crossed = lane < 16 if step_y == 1 else lane >= 112
        moved = [
            {t: jnp.where(crossed, moved[k][(t - step_y) % 3], moved[k][t]) for t in tiles}
            for k in range(2)
        ]
    return moved


def advance(col, xg, yg, cp, tab, out, ext, nxt, ux, fs):
    me_x = lax.axis_index("bx")
    side = lax.rem(me_x, 2)
    mate = me_x + 1 - 2 * side

    def bit(table, device, k):
        row = tab[table]
        hit = (lanes_of(row.shape) == device) & (lax.broadcasted_iota(jnp.int32, row.shape, 0) == k)
        return jnp.sum(jnp.where(hit, row, 0).astype(F32))

    own_live = [bit(0, me_x, k) for k in range(2)]
    own_moving = [bit(1, me_x, k) for k in range(2)]
    arriving = [bit(1, mate, k) for k in range(2)]
    swap = (own_live[0] + own_live[1] < 0.5) & (arriving[0] + arriving[1] > 0.5)
    chosen = [
        jnp.where(swap, arriving[k], own_live[k] * (1.0 - own_moving[k])) > 0.5 for k in range(2)
    ]
    sc = jnp.where(swap, 1 - side, side)

    outer_near, outer_far = 7 + 17 * sc, 6 + 19 * sc
    inner_near, inner_far = 24 - 17 * sc, 25 - 19 * sc
    mate_near, mate_far = 15 * sc, 1 + 13 * sc
    lane8 = lanes_of((8, 128))

    def place_outer(k, tile, planes):
        ext[k, tile, pl.ds(outer_near, 19, stride=32), :] = planes[0:19, :]
        ext[k, tile, pl.ds((1 + sc) * 32 + outer_far, 1), :] = planes[19:20, :]
        ext[k, tile, pl.ds((7 + sc) * 32 + outer_far, 4, stride=64), :] = planes[20:24, :]

    for k in range(2):
        for tile in range(2):
            for q in range(19):
                ext[k, tile, q * 32 + 8 : q * 32 + 24, :] = col[sc, k, tile, q * 16 : q * 16 + 16, :]
            place_outer(k, tile, xg.at[sc, tile, k])
            ext[k, tile, pl.ds(inner_near, 19, stride=32), :] = col[
                1 - sc, k, tile, pl.ds(mate_near, 19, stride=16), :
            ]
            ext[k, tile, pl.ds(inner_far, 19, stride=32), :] = col[
                1 - sc, k, tile, pl.ds(mate_far, 19, stride=16), :
            ]
        for g in range(3):
            low = cp[0, sc, k]
            high = cp[1, sc, k]
            low = pltpu.roll(low, (96 - 32 * g) % 128, 1)
            high = pltpu.roll(high, (-32 * g) % 128, 1) if g else high
            ux[k, 8 * g : 8 * g + 8, :] = jnp.where(lane8 < 64, high, low)
        place_outer(k, 2, ux.at[k])

        for own in range(2):
            rows = 16 if own else 8
            lane = lanes_of((rows, 128))
            for q in range(19):
                parts = []
                for way in range(2):
                    near_lane, far_lane = ((112, 96), (0, 16))[way]

                    def unit(p, lane_to, way=way):
                        if own:
                            value = yg[way, sc, k, p // 8]
                        else:
                            value = yg[way, 1 - sc, k, p // 8, pl.ds(pl.multiple_of(8 * sc, 8), 8), :]
                        shift = (lane_to - 16 * (p % 8)) % 128
                        return pltpu.roll(value, shift, 1) if shift else value

                    value = unit(q, near_lane)
                    if q in RING_Y[way]:
                        far = unit(19 + RING_Y[way].index(q), far_lane)
                        value = jnp.where(lane // 16 == near_lane // 16, value, far)
                    parts.append(value)
                value = jnp.where(lane < 64, parts[1], parts[0])
                if own:
                    ext[k, 2, q * 32 + 8 : q * 32 + 24, :] = value
                else:
                    ext[k, 2, pl.ds(pl.multiple_of(q * 32 + 24 - 24 * sc, 8), 8), :] = value

    def arrive(source, stride, base, q, row, tiles):
        moved = stream(source, q, q * stride + base + row - VELOCITIES[q][0], tiles)
        result = {}
        for k in range(2):
            for t in tiles:
                value = moved[k][t]
                if q:
                    back = source[k, t, pl.ds(OPPOSITE[q] * stride + base + row, 8), :]
                    value = jnp.where(value > SOLID_TEST, value, back)
                result[k, t] = value
        return result

    for chunk in range(3):
        for q in range(19):
            for (k, t), value in arrive(ext, 32, 7, q, 8 * chunk, (0, 1, 2)).items():
                fs[q, k, t] = value
        for k in range(2):
            for t in range(3):
                f = [fs[q, k, t] for q in range(19)]
                fluid = f[0] > SOLID_TEST
                for q, value in enumerate(collide(f)):
                    nxt[k, t, q * 24 + 8 * chunk : q * 24 + 8 * chunk + 8, :] = jnp.where(
                        fluid, value, SOLID
                    )

    zero = jnp.zeros((8, 128), F32)
    both = chosen[0] & chosen[1]
    for chunk in range(2):
        for q in range(19):
            values = arrive(nxt, 24, 1, q, 8 * chunk, (0, 1))
            for t in range(2):
                spot = (q, slice(8 * chunk, 8 * chunk + 8), slice(128 * t, 128 * t + 128))
                lower, upper = values[0, t], values[1, t]
                out[(0,) + spot] = jnp.where(chosen[0], lower, jnp.where(chosen[1], upper, zero))
                out[(1,) + spot] = jnp.where(both, upper, zero)


VMEM = pl.BlockSpec(memory_space=pltpu.VMEM)
HBM = pl.BlockSpec(memory_space=pltpu.HBM)


def shards(n_x, n_y, populations, live_blocks, moving):
    pop, live, move = (
        pltpu.with_memory_space_constraint(array, pltpu.HBM)
        for array in (
            populations.reshape(2, 19, 16, 256),
            jnp.transpose(live_blocks, (1, 2, 0)),
            jnp.transpose(moving, (1, 2, 0)),
        )
    )
    shapes = [(2, 2, 2, 304, 128), (2, 2, 2, 24, 128), (2, 2, 2, 3, 16, 128), (2, 2, 2, 8, 128)]
    parts = pl.pallas_call(
        functools.partial(exchange, n_x, n_y),
        out_shape=[jax.ShapeDtypeStruct(shape, F32) for shape in shapes]
        + [jax.ShapeDtypeStruct((2, 2, n_x), jnp.int32)],
        in_specs=[HBM] * 3,
        out_specs=[VMEM] * 5,
        scratch_shapes=[
            pltpu.VMEM((2, 2, 19, 16, 256), F32),
            pltpu.VMEM((2, 2, 2, 24, 128), F32),
            pltpu.VMEM((2, 2, 2, 3, 16, 128), F32),
            pltpu.VMEM((2, 2, 2, 8, 128), F32),
            pltpu.SemaphoreType.DMA((3,)),
            pltpu.SemaphoreType.DMA((11,)),
            pltpu.SemaphoreType.DMA((11,)),
            pltpu.SemaphoreType.REGULAR,
        ],
        compiler_params=pltpu.CompilerParams(
            collective_id=0, has_side_effects=True, vmem_limit_bytes=8 << 20
        ),
        name="exchange",
    )(pop, live, move)
    result = pl.pallas_call(
        advance,
        out_shape=jax.ShapeDtypeStruct((2, 19, 16, 256), F32),
        in_specs=[VMEM] * 5,
        out_specs=VMEM,
        scratch_shapes=[
            pltpu.VMEM((2, 3, 19 * 32, 128), F32),
            pltpu.VMEM((2, 3, 19 * 24, 128), F32),
            pltpu.VMEM((2, 24, 128), F32),
            pltpu.VMEM((19, 2, 3, 8, 128), F32),
        ],
        compiler_params=pltpu.CompilerParams(vmem_limit_bytes=12 << 20),
        name="advance",
    )(*parts)
    return result.reshape(1, 1, 2, 19, 16, 256)


def solution(mesh):
    n_x, n_y = mesh.shape["bx"], mesh.shape["by"]
    placed = (P("bx", "by", None, None, None, None), P(), P())
    return jax.shard_map(
        functools.partial(shards, n_x, n_y),
        mesh=mesh,
        in_specs=placed,
        out_specs=P("bx", "by", None, None, None, None),
        check_vma=False,
    )
```

```python
import functools

import jax
import jax.numpy as jnp
from jax import lax
from jax.experimental import pallas as pl
from jax.experimental.pallas import tpu as pltpu
from jax.sharding import PartitionSpec as P

MESH = pl.DeviceIdType.MESH
VELOCITIES = [
    (0, 0, 0), (1, 0, 0), (-1, 0, 0), (0, 1, 0), (0, -1, 0), (0, 0, 1), (0, 0, -1),
    (1, 1, 0), (-1, -1, 0), (1, -1, 0), (-1, 1, 0), (1, 0, 1), (-1, 0, -1),
    (1, 0, -1), (-1, 0, 1), (0, 1, 1), (0, -1, -1), (0, 1, -1), (0, -1, 1),
]
OPPOSITE = [0, 2, 1, 4, 3, 6, 5, 8, 7, 10, 9, 12, 11, 14, 13, 16, 15, 18, 17]
SMAG_COEF = 18.0 * 2.0**0.5 * 0.17**2
SOLID = -1e30
SOLID_TEST = -1e29
RING_Y = ([3, 7, 10, 15, 17], [4, 8, 9, 16, 18])
F32 = jnp.float32


def collide(f):
    sums, diffs = {}, {}
    for i in range(1, 19, 2):
        sums[i] = f[i] + f[i + 1]
        diffs[i] = f[i] - f[i + 1]
    side_xy = sums[7] + sums[9]
    side_xz = sums[11] + sums[13]
    side_yz = sums[15] + sums[17]
    density = f[0] + (sums[1] + sums[3] + sums[5]) + (side_xy + side_xz + side_yz)
    mom_x = diffs[1] + (diffs[7] + diffs[9]) + (diffs[11] + diffs[13])
    mom_y = diffs[3] + (diffs[7] - diffs[9]) + (diffs[15] + diffs[17])
    mom_z = diffs[5] + (diffs[11] - diffs[13]) + (diffs[15] - diffs[17])
    inverse = 1.0 / density
    vel_x, vel_y, vel_z = mom_x * inverse, mom_y * inverse, mom_z * inverse
    third = density * (1.0 / 3.0)
    p_xx = sums[1] + side_xy + side_xz - third - mom_x * vel_x
    p_yy = sums[3] + side_xy + side_yz - third - mom_y * vel_y
    p_zz = sums[5] + side_xz + side_yz - third - mom_z * vel_z
    p_xy = sums[7] - sums[9] - mom_x * vel_y
    p_xz = sums[11] - sums[13] - mom_x * vel_z
    p_yz = sums[15] - sums[17] - mom_y * vel_z
    strength = jnp.sqrt(
        p_xx * p_xx + p_yy * p_yy + p_zz * p_zz + 2.0 * (p_xy * p_xy + p_xz * p_xz + p_yz * p_yz)
    )
    omega = 2.0 / (0.6 + jnp.sqrt(0.36 + SMAG_COEF * strength * inverse))
    keep = 1.0 - omega
    gain = omega * density
    speed = vel_x * vel_x + vel_y * vel_y + vel_z * vel_z
    base = 1.0 - 1.5 * speed
    edge, corner = gain * (1.0 / 18.0), gain * (1.0 / 36.0)
    base_edge, base_corner = edge * base, corner * base
    result = [None] * 19
    result[0] = f[0] * keep + (gain * (1.0 / 3.0)) * base
    along = {
        1: vel_x, 3: vel_y, 5: vel_z,
        7: vel_x + vel_y, 9: vel_x - vel_y, 11: vel_x + vel_z,
        13: vel_x - vel_z, 15: vel_y + vel_z, 17: vel_y - vel_z,
    }
    for i in range(1, 19, 2):
        weight, rest = (edge, base_edge) if i < 7 else (corner, base_corner)
        odd = 3.0 * weight * along[i]
        even = rest + (1.5 * odd) * along[i]
        result[i] = f[i] * keep + (even + odd)
        result[i + 1] = f[i + 1] * keep + (even - odd)
    return result


def lanes_of(shape):
    return lax.broadcasted_iota(jnp.int32, shape, len(shape) - 1)


def exchange(
    n_x, n_y, pop, live, move, col, xg, yg, cp, tab,
    fbuf, xs, ys, cs, in_sem, send_sem, recv_sem, allowed,
):
    me_x, me_y = lax.axis_index("bx"), lax.axis_index("by")
    side = lax.rem(me_x, 2)
    base = me_x - side
    hub = base + 1
    at_mate = (base + 1 - side, me_y)
    prev_hub = lax.rem(base + n_x - 1, n_x)
    next_hub = lax.rem(base + 3, n_x)
    next_zero = lax.rem(base + 2, n_x)
    rows_y = (lax.rem(me_y + 1, n_y), lax.rem(me_y + n_y - 1, n_y))
    barrier = pltpu.get_barrier_semaphore()

    def greet(semaphore, devices):
        for device in devices:
            pl.semaphore_signal(semaphore, inc=1, device_id=device, device_id_type=MESH)

    @pl.when(side == 1)
    def _():
        around = (me_y,) + rows_y
        greet(barrier, [(prev_hub, y) for y in around] + [(hub, y) for y in rows_y] + [(next_zero, y) for y in around])

    @pl.when(side == 0)
    def _():
        greet(barrier, [at_mate])

    load_pop = pltpu.make_async_copy(pop, fbuf.at[side], in_sem.at[0])
    load_live = pltpu.make_async_copy(live.at[me_y], tab.at[0], in_sem.at[1])
    load_move = pltpu.make_async_copy(move.at[me_y], tab.at[1], in_sem.at[2])
    load_pop.start()
    load_live.start()
    load_move.start()

    def link(index, source, target, device):
        return pltpu.make_async_remote_copy(
            src_ref=source,
            dst_ref=target,
            send_sem=send_sem.at[index],
            recv_sem=recv_sem.at[index],
            device_id=device,
            device_id_type=MESH,
        )

    raw = link(0, pop, fbuf.at[side], at_mate)
    high = link(1, xs.at[1], xg.at[0], (next_hub, me_y))
    low = link(2, xs.at[0], xg.at[1], (prev_hub, me_y))
    high_corner = [link(3 + w, cs.at[w, 1], cp.at[w, 0], (next_hub, rows_y[w])) for w in range(2)]
    low_corner = [link(5 + w, cs.at[w, 0], cp.at[w, 1], (prev_hub, rows_y[w])) for w in range(2)]
    face = [
        [link(7 + 2 * w + c, ys.at[w, c], yg.at[w, c], (hub, rows_y[w])) for w in range(2)] for c in range(2)
    ]
    relay_x = link(11, xg, xg, at_mate)
    relay_y = [link(12 + w, yg.at[w], yg.at[w], at_mate) for w in range(2)]
    relay_c = [link(14 + w, cp.at[w], cp.at[w], at_mate) for w in range(2)]

    load_live.wait()
    load_move.wait()
    load_pop.wait()

    def relax_column(c):
        row = tab[0]
        hit = lanes_of(row.shape) == base + c
        flags = jnp.sum(jnp.where(hit, row, 0).astype(F32), axis=1, keepdims=True)
        first = jnp.broadcast_to(flags[0:1, :], (8, 128)) > 0.5
        second = jnp.broadcast_to(flags[1:2, :], (8, 128)) > 0.5
        for k in range(2):
            fluid = (first, second)[k]

            def relax(i, carry, k=k, fluid=fluid):
                tile, half = i // 2, i % 2
                rows = pl.ds(pl.multiple_of(half * 8, 8), 8)
                lanes = pl.ds(pl.multiple_of(tile * 128, 128), 128)
                f = [
                    jnp.where(first, fbuf[c, k, q, rows, lanes], fbuf[c, 1 - k, q, rows, lanes])
                    for q in range(19)
                ]
                for q, value in enumerate(collide(f)):
                    to = pl.ds(pl.multiple_of(q * 16 + half * 8, 8), 8)
                    col[c, k, tile, to, :] = jnp.where(fluid, value, SOLID)
                return carry

            lax.fori_loop(0, 4, relax, 0)

    group = lanes_of((16, 128)) // 16
    quarter = lanes_of((8, 128)) // 32

    def pack_x(c):
        near, far = 15 * c, 1 + 13 * c
        for tile in range(2):
            for k in range(2):
                own = col.at[c, k, tile]
                xs[c, tile, k, 0:19, :] = own[pl.ds(near, 19, stride=16), :]
                xs[c, tile, k, 19:20, :] = own[pl.ds((2 - c) * 16 + far, 1), :]
                xs[c, tile, k, 20:24, :] = own[pl.ds((8 - c) * 16 + far, 4, stride=32), :]
        for way in range(2):
            for k in range(2):
                packed = None
                for g in range(3):
                    value = xs[c, 1 - way, k, 8 * g : 8 * g + 8, :]
                    shift = (32 * g - (96, 0)[way]) % 128
                    if shift:
                        value = pltpu.roll(value, shift, 1)
                    packed = value if packed is None else jnp.where(quarter == g, value, packed)
                cs[way, c, k] = packed

    def pack_y(c):
        def pack(k, carry):
            for way in range(2):
                tile, first_lane, second_lane = ((1, 112, 96), (0, 0, 16))[way]
                for g in range(3):
                    packed = None
                    for i in range(8):
                        p = 8 * g + i
                        q, lane = (p, first_lane) if p < 19 else (RING_Y[way][p - 19], second_lane)
                        value = col[c, k, tile, q * 16 : q * 16 + 16, :]
                        shift = (16 * i - lane) % 128
                        if shift:
                            value = pltpu.roll(value, shift, 1)
                        packed = value if packed is None else jnp.where(group == i, value, packed)
                    ys[way, c, k, g] = packed
            return carry

        lax.fori_loop(0, 2, pack, 0)

    relax_column(side)

    @pl.when(side == 1)
    def _():
        pack_x(1)
        pack_y(1)
        pl.semaphore_wait(barrier, 6)
        greet(allowed, [at_mate])
        for copy in high_corner + face[1] + [high, raw]:
            copy.start()

    @pl.when(side == 0)
    def _():
        pack_x(0)
        pl.semaphore_wait(allowed, 1)
        raw.start()
        pl.semaphore_wait(barrier, 3)
        for copy in low_corner + [low]:
            copy.start()

    raw.wait_recv()
    relax_column(1 - side)

    @pl.when(side == 1)
    def _():
        pack_y(0)
        for copy in face[0]:
            copy.start()
        high.wait_recv()
        low.wait_recv()
        relay_x.start()
        for w in range(2):
            face[1][w].wait_recv()
            face[0][w].wait_recv()
            relay_y[w].start()
        for w in range(2):
            high_corner[w].wait_recv()
            low_corner[w].wait_recv()
            relay_c[w].start()
        for copy in high_corner + face[0] + face[1] + [high, relay_x] + relay_y + relay_c:
            copy.wait_send()

    @pl.when(side == 0)
    def _():
        for copy in [relay_x] + relay_y + relay_c:
            copy.wait_recv()
        for copy in low_corner + [low]:
            copy.wait_send()

    raw.wait_send()


def stream(source, q, row, tiles):
    _, step_y, step_z = VELOCITIES[q]
    need = sorted({(t - d) % 3 for t in tiles for d in ((0, step_y) if step_y else (0,))})
    data = [{t: source[k, t, pl.ds(row, 8), :] for t in need} for k in range(2)]
    lane = lanes_of((8, 128))

    def turn(value, shift):
        return pltpu.roll(value, shift % 128, 1) if shift % 128 else value

    if step_z:
        at_edge = lane % 16 == (0 if step_z == 1 else 15)
        moved = [
            {
                t: jnp.where(
                    at_edge,
                    turn(data[1 - k][t], 16 * step_y - 15 * step_z),
                    turn(data[k][t], 16 * step_y + step_z),
                )
                for t in need
            }
            for k in range(2)
        ]
    else:
        moved = [{t: turn(data[k][t], 16 * step_y) for t in need} for k in range(2)]
    if step_y:
        crossed = lane < 16 if step_y == 1 else lane >= 112
        moved = [
            {t: jnp.where(crossed, moved[k][(t - step_y) % 3], moved[k][t]) for t in tiles}
            for k in range(2)
        ]
    return moved


def advance(col, xg, yg, cp, tab, out, ext, nxt, ux, fs):
    me_x = lax.axis_index("bx")
    side = lax.rem(me_x, 2)
    mate = me_x + 1 - 2 * side

    def bit(table, device, k):
        row = tab[table]
        hit = (lanes_of(row.shape) == device) & (lax.broadcasted_iota(jnp.int32, row.shape, 0) == k)
        return jnp.sum(jnp.where(hit, row, 0).astype(F32))

    own_live = [bit(0, me_x, k) for k in range(2)]
    own_moving = [bit(1, me_x, k) for k in range(2)]
    arriving = [bit(1, mate, k) for k in range(2)]
    swap = (own_live[0] + own_live[1] < 0.5) & (arriving[0] + arriving[1] > 0.5)
    chosen = [
        jnp.where(swap, arriving[k], own_live[k] * (1.0 - own_moving[k])) > 0.5 for k in range(2)
    ]
    sc = jnp.where(swap, 1 - side, side)

    outer_near, outer_far = 7 + 17 * sc, 6 + 19 * sc
    inner_near, inner_far = 24 - 17 * sc, 25 - 19 * sc
    mate_near, mate_far = 15 * sc, 1 + 13 * sc
    lane8 = lanes_of((8, 128))

    def place_outer(k, tile, planes):
        ext[k, tile, pl.ds(outer_near, 19, stride=32), :] = planes[0:19, :]
        ext[k, tile, pl.ds((1 + sc) * 32 + outer_far, 1), :] = planes[19:20, :]
        ext[k, tile, pl.ds((7 + sc) * 32 + outer_far, 4, stride=64), :] = planes[20:24, :]

    for k in range(2):
        for tile in range(2):
            for q in range(19):
                ext[k, tile, q * 32 + 8 : q * 32 + 24, :] = col[sc, k, tile, q * 16 : q * 16 + 16, :]
            place_outer(k, tile, xg.at[sc, tile, k])
            ext[k, tile, pl.ds(inner_near, 19, stride=32), :] = col[
                1 - sc, k, tile, pl.ds(mate_near, 19, stride=16), :
            ]
            ext[k, tile, pl.ds(inner_far, 19, stride=32), :] = col[
                1 - sc, k, tile, pl.ds(mate_far, 19, stride=16), :
            ]
        for g in range(3):
            low = cp[0, sc, k]
            high = cp[1, sc, k]
            low = pltpu.roll(low, (96 - 32 * g) % 128, 1)
            high = pltpu.roll(high, (-32 * g) % 128, 1) if g else high
            ux[k, 8 * g : 8 * g + 8, :] = jnp.where(lane8 < 64, high, low)
        place_outer(k, 2, ux.at[k])

        for own in range(2):
            rows = 16 if own else 8
            lane = lanes_of((rows, 128))
            for q in range(19):
                parts = []
                for way in range(2):
                    near_lane, far_lane = ((112, 96), (0, 16))[way]

                    def unit(p, lane_to, way=way):
                        if own:
                            value = yg[way, sc, k, p // 8]
                        else:
                            value = yg[way, 1 - sc, k, p // 8, pl.ds(pl.multiple_of(8 * sc, 8), 8), :]
                        shift = (lane_to - 16 * (p % 8)) % 128
                        return pltpu.roll(value, shift, 1) if shift else value

                    value = unit(q, near_lane)
                    if q in RING_Y[way]:
                        far = unit(19 + RING_Y[way].index(q), far_lane)
                        value = jnp.where(lane // 16 == near_lane // 16, value, far)
                    parts.append(value)
                value = jnp.where(lane < 64, parts[1], parts[0])
                if own:
                    ext[k, 2, q * 32 + 8 : q * 32 + 24, :] = value
                else:
                    ext[k, 2, pl.ds(pl.multiple_of(q * 32 + 24 - 24 * sc, 8), 8), :] = value

    def arrive(source, stride, base, q, row, tiles):
        moved = stream(source, q, q * stride + base + row - VELOCITIES[q][0], tiles)
        result = {}
        for k in range(2):
            for t in tiles:
                value = moved[k][t]
                if q:
                    back = source[k, t, pl.ds(OPPOSITE[q] * stride + base + row, 8), :]
                    value = jnp.where(value > SOLID_TEST, value, back)
                result[k, t] = value
        return result

    for chunk in range(3):
        for q in range(19):
            for (k, t), value in arrive(ext, 32, 7, q, 8 * chunk, (0, 1, 2)).items():
                fs[q, k, t] = value
        for k in range(2):
            for t in range(3):
                f = [fs[q, k, t] for q in range(19)]
                fluid = f[0] > SOLID_TEST
                for q, value in enumerate(collide(f)):
                    nxt[k, t, q * 24 + 8 * chunk : q * 24 + 8 * chunk + 8, :] = jnp.where(
                        fluid, value, SOLID
                    )

    zero = jnp.zeros((8, 128), F32)
    both = chosen[0] & chosen[1]
    for chunk in range(2):
        for q in range(19):
            values = arrive(nxt, 24, 1, q, 8 * chunk, (0, 1))
            for t in range(2):
                spot = (q, slice(8 * chunk, 8 * chunk + 8), slice(128 * t, 128 * t + 128))
                lower, upper = values[0, t], values[1, t]
                out[(0,) + spot] = jnp.where(chosen[0], lower, jnp.where(chosen[1], upper, zero))
                out[(1,) + spot] = jnp.where(both, upper, zero)


VMEM = pl.BlockSpec(memory_space=pltpu.VMEM)
HBM = pl.BlockSpec(memory_space=pltpu.HBM)


def shards(n_x, n_y, populations, live_blocks, moving):
    pop, live, move = (
        pltpu.with_memory_space_constraint(array, pltpu.HBM)
        for array in (
            populations.reshape(2, 19, 16, 256),
            jnp.transpose(live_blocks, (1, 2, 0)),
            jnp.transpose(moving, (1, 2, 0)),
        )
    )
    shapes = [(2, 2, 2, 304, 128), (2, 2, 2, 24, 128), (2, 2, 2, 3, 16, 128), (2, 2, 2, 8, 128)]
    parts = pl.pallas_call(
        functools.partial(exchange, n_x, n_y),
        out_shape=[jax.ShapeDtypeStruct(shape, F32) for shape in shapes]
        + [jax.ShapeDtypeStruct((2, 2, n_x), jnp.int32)],
        in_specs=[HBM] * 3,
        out_specs=[VMEM] * 5,
        scratch_shapes=[
            pltpu.VMEM((2, 2, 19, 16, 256), F32),
            pltpu.VMEM((2, 2, 2, 24, 128), F32),
            pltpu.VMEM((2, 2, 2, 3, 16, 128), F32),
            pltpu.VMEM((2, 2, 2, 8, 128), F32),
            pltpu.SemaphoreType.DMA((3,)),
            pltpu.SemaphoreType.DMA((16,)),
            pltpu.SemaphoreType.DMA((16,)),
            pltpu.SemaphoreType.REGULAR,
        ],
        compiler_params=pltpu.CompilerParams(
            collective_id=0, has_side_effects=True, vmem_limit_bytes=8 << 20
        ),
        name="exchange",
    )(pop, live, move)
    result = pl.pallas_call(
        advance,
        out_shape=jax.ShapeDtypeStruct((2, 19, 16, 256), F32),
        in_specs=[VMEM] * 5,
        out_specs=VMEM,
        scratch_shapes=[
            pltpu.VMEM((2, 3, 19 * 32, 128), F32),
            pltpu.VMEM((2, 3, 19 * 24, 128), F32),
            pltpu.VMEM((2, 24, 128), F32),
            pltpu.VMEM((19, 2, 3, 8, 128), F32),
        ],
        compiler_params=pltpu.CompilerParams(vmem_limit_bytes=12 << 20),
        name="advance",
    )(*parts)
    return result.reshape(1, 1, 2, 19, 16, 256)


def solution(mesh):
    n_x, n_y = mesh.shape["bx"], mesh.shape["by"]
    placed = (P("bx", "by", None, None, None, None), P(), P())
    return jax.shard_map(
        functools.partial(shards, n_x, n_y),
        mesh=mesh,
        in_specs=placed,
        out_specs=P("bx", "by", None, None, None, None),
        check_vma=False,
    )
```

```python
import functools

import jax
import jax.numpy as jnp
from jax import lax
from jax.experimental import pallas as pl
from jax.experimental.pallas import tpu as pltpu
from jax.sharding import PartitionSpec as P

MESH = pl.DeviceIdType.MESH
VELOCITIES = [
    (0, 0, 0), (1, 0, 0), (-1, 0, 0), (0, 1, 0), (0, -1, 0), (0, 0, 1), (0, 0, -1),
    (1, 1, 0), (-1, -1, 0), (1, -1, 0), (-1, 1, 0), (1, 0, 1), (-1, 0, -1),
    (1, 0, -1), (-1, 0, 1), (0, 1, 1), (0, -1, -1), (0, 1, -1), (0, -1, 1),
]
OPPOSITE = [0, 2, 1, 4, 3, 6, 5, 8, 7, 10, 9, 12, 11, 14, 13, 16, 15, 18, 17]
SMAG_COEF = 18.0 * 2.0**0.5 * 0.17**2
SOLID = -1e30
SOLID_TEST = -1e29
RING_Y = ([3, 7, 10, 15, 17], [4, 8, 9, 16, 18])
F32 = jnp.float32


def collide(f):
    sums, diffs = {}, {}
    for i in range(1, 19, 2):
        sums[i] = f[i] + f[i + 1]
        diffs[i] = f[i] - f[i + 1]
    side_xy = sums[7] + sums[9]
    side_xz = sums[11] + sums[13]
    side_yz = sums[15] + sums[17]
    density = f[0] + (sums[1] + sums[3] + sums[5]) + (side_xy + side_xz + side_yz)
    mom_x = diffs[1] + (diffs[7] + diffs[9]) + (diffs[11] + diffs[13])
    mom_y = diffs[3] + (diffs[7] - diffs[9]) + (diffs[15] + diffs[17])
    mom_z = diffs[5] + (diffs[11] - diffs[13]) + (diffs[15] - diffs[17])
    inverse = 1.0 / density
    vel_x, vel_y, vel_z = mom_x * inverse, mom_y * inverse, mom_z * inverse
    third = density * (1.0 / 3.0)
    p_xx = sums[1] + side_xy + side_xz - third - mom_x * vel_x
    p_yy = sums[3] + side_xy + side_yz - third - mom_y * vel_y
    p_zz = sums[5] + side_xz + side_yz - third - mom_z * vel_z
    p_xy = sums[7] - sums[9] - mom_x * vel_y
    p_xz = sums[11] - sums[13] - mom_x * vel_z
    p_yz = sums[15] - sums[17] - mom_y * vel_z
    strength = jnp.sqrt(
        p_xx * p_xx + p_yy * p_yy + p_zz * p_zz + 2.0 * (p_xy * p_xy + p_xz * p_xz + p_yz * p_yz)
    )
    omega = 2.0 / (0.6 + jnp.sqrt(0.36 + SMAG_COEF * strength * inverse))
    keep = 1.0 - omega
    gain = omega * density
    speed = vel_x * vel_x + vel_y * vel_y + vel_z * vel_z
    base = 1.0 - 1.5 * speed
    edge, corner = gain * (1.0 / 18.0), gain * (1.0 / 36.0)
    base_edge, base_corner = edge * base, corner * base
    result = [None] * 19
    result[0] = f[0] * keep + (gain * (1.0 / 3.0)) * base
    along = {
        1: vel_x, 3: vel_y, 5: vel_z,
        7: vel_x + vel_y, 9: vel_x - vel_y, 11: vel_x + vel_z,
        13: vel_x - vel_z, 15: vel_y + vel_z, 17: vel_y - vel_z,
    }
    for i in range(1, 19, 2):
        weight, rest = (edge, base_edge) if i < 7 else (corner, base_corner)
        odd = 3.0 * weight * along[i]
        even = rest + (1.5 * odd) * along[i]
        result[i] = f[i] * keep + (even + odd)
        result[i + 1] = f[i + 1] * keep + (even - odd)
    return result


def lanes_of(shape):
    return lax.broadcasted_iota(jnp.int32, shape, len(shape) - 1)


def exchange(
    n_x, n_y, pop, live, move, col, xg, yg, cp, tab,
    fbuf, xs, ys, cs, in_sem, send_sem, recv_sem, allowed,
):
    me_x, me_y = lax.axis_index("bx"), lax.axis_index("by")
    side = lax.rem(me_x, 2)
    base = me_x - side
    hub = base + 1
    at_mate = (base + 1 - side, me_y)
    prev_hub = lax.rem(base + n_x - 1, n_x)
    next_hub = lax.rem(base + 3, n_x)
    next_zero = lax.rem(base + 2, n_x)
    rows_y = (lax.rem(me_y + 1, n_y), lax.rem(me_y + n_y - 1, n_y))
    barrier = pltpu.get_barrier_semaphore()

    def greet(semaphore, devices):
        for device in devices:
            pl.semaphore_signal(semaphore, inc=1, device_id=device, device_id_type=MESH)

    @pl.when(side == 1)
    def _():
        around = (me_y,) + rows_y
        greet(barrier, [(prev_hub, y) for y in around] + [(hub, y) for y in rows_y] + [(next_zero, y) for y in around])

    @pl.when(side == 0)
    def _():
        greet(barrier, [at_mate])

    load_pop = pltpu.make_async_copy(pop, fbuf.at[side], in_sem.at[0])
    load_live = pltpu.make_async_copy(live.at[me_y], tab.at[0], in_sem.at[1])
    load_move = pltpu.make_async_copy(move.at[me_y], tab.at[1], in_sem.at[2])
    load_pop.start()
    load_live.start()
    load_move.start()

    def link(index, source, target, device):
        return pltpu.make_async_remote_copy(
            src_ref=source,
            dst_ref=target,
            send_sem=send_sem.at[index],
            recv_sem=recv_sem.at[index],
            device_id=device,
            device_id_type=MESH,
        )

    raw = link(0, pop, fbuf.at[side], at_mate)
    high = link(1, xs.at[1], xg.at[0], (next_hub, me_y))
    low = link(2, xs.at[0], xg.at[1], (prev_hub, me_y))
    high_corner = [link(3 + w, cs.at[w, 1], cp.at[w, 0], (next_hub, rows_y[w])) for w in range(2)]
    low_corner = [link(5 + w, cs.at[w, 0], cp.at[w, 1], (prev_hub, rows_y[w])) for w in range(2)]
    face = [
        [link(7 + 2 * w + c, ys.at[w, c], yg.at[w, c], (hub, rows_y[w])) for w in range(2)] for c in range(2)
    ]
    relay_x = link(11, xg, xg, at_mate)
    relay_y = [link(12 + w, yg.at[w], yg.at[w], at_mate) for w in range(2)]
    relay_c = [link(14 + w, cp.at[w], cp.at[w], at_mate) for w in range(2)]

    load_live.wait()
    load_move.wait()
    load_pop.wait()

    def relax_column(c):
        row = tab[0]
        hit = lanes_of(row.shape) == base + c
        flags = jnp.sum(jnp.where(hit, row, 0).astype(F32), axis=1, keepdims=True)
        first = jnp.broadcast_to(flags[0:1, :], (8, 128)) > 0.5
        second = jnp.broadcast_to(flags[1:2, :], (8, 128)) > 0.5
        for k in range(2):
            fluid = (first, second)[k]

            def relax(i, carry, k=k, fluid=fluid):
                tile, half = i // 2, i % 2
                rows = pl.ds(pl.multiple_of(half * 8, 8), 8)
                lanes = pl.ds(pl.multiple_of(tile * 128, 128), 128)
                f = [
                    jnp.where(first, fbuf[c, k, q, rows, lanes], fbuf[c, 1 - k, q, rows, lanes])
                    for q in range(19)
                ]
                for q, value in enumerate(collide(f)):
                    to = pl.ds(pl.multiple_of(q * 16 + half * 8, 8), 8)
                    col[c, k, tile, to, :] = jnp.where(fluid, value, SOLID)
                return carry

            lax.fori_loop(0, 4, relax, 0)

    group = lanes_of((16, 128)) // 16
    quarter = lanes_of((8, 128)) // 32

    def pack_x(c):
        near, far = 15 * c, 1 + 13 * c
        for tile in range(2):
            for k in range(2):
                own = col.at[c, k, tile]
                xs[c, tile, k, 0:19, :] = own[pl.ds(near, 19, stride=16), :]
                xs[c, tile, k, 19:20, :] = own[pl.ds((2 - c) * 16 + far, 1), :]
                xs[c, tile, k, 20:24, :] = own[pl.ds((8 - c) * 16 + far, 4, stride=32), :]
        for way in range(2):
            for k in range(2):
                packed = None
                for g in range(3):
                    value = xs[c, 1 - way, k, 8 * g : 8 * g + 8, :]
                    shift = (32 * g - (96, 0)[way]) % 128
                    if shift:
                        value = pltpu.roll(value, shift, 1)
                    packed = value if packed is None else jnp.where(quarter == g, value, packed)
                cs[way, c, k] = packed

    def pack_y(c):
        def pack(k, carry):
            for way in range(2):
                tile, first_lane, second_lane = ((1, 112, 96), (0, 0, 16))[way]
                for g in range(3):
                    packed = None
                    for i in range(8):
                        p = 8 * g + i
                        q, lane = (p, first_lane) if p < 19 else (RING_Y[way][p - 19], second_lane)
                        value = col[c, k, tile, q * 16 : q * 16 + 16, :]
                        shift = (16 * i - lane) % 128
                        if shift:
                            value = pltpu.roll(value, shift, 1)
                        packed = value if packed is None else jnp.where(group == i, value, packed)
                    ys[way, c, k, g] = packed
            return carry

        lax.fori_loop(0, 2, pack, 0)

    relax_column(side)

    @pl.when(side == 1)
    def _():
        pack_x(1)
        pl.semaphore_wait(barrier, 6)
        greet(allowed, [at_mate])
        for copy in high_corner + [high]:
            copy.start()
        pack_y(1)
        for copy in face[1] + [raw]:
            copy.start()

    @pl.when(side == 0)
    def _():
        pack_x(0)
        pack_y(0)
        pl.semaphore_wait(allowed, 1)
        for copy in face[0] + [raw]:
            copy.start()
        pl.semaphore_wait(barrier, 3)
        for copy in low_corner + [low]:
            copy.start()

    raw.wait_recv()
    relax_column(1 - side)

    @pl.when(side == 1)
    def _():
        high.wait_recv()
        low.wait_recv()
        relay_x.start()
        for w in range(2):
            face[1][w].wait_recv()
            face[0][w].wait_recv()
            relay_y[w].start()
        for w in range(2):
            high_corner[w].wait_recv()
            low_corner[w].wait_recv()
            relay_c[w].start()
        for copy in high_corner + face[1] + [high, relay_x] + relay_y + relay_c:
            copy.wait_send()

    @pl.when(side == 0)
    def _():
        for copy in [relay_x] + relay_y + relay_c:
            copy.wait_recv()
        for copy in low_corner + face[0] + [low]:
            copy.wait_send()

    raw.wait_send()


def stream(source, q, row, tiles):
    _, step_y, step_z = VELOCITIES[q]
    need = sorted({(t - d) % 3 for t in tiles for d in ((0, step_y) if step_y else (0,))})
    data = [{t: source[k, t, pl.ds(row, 8), :] for t in need} for k in range(2)]
    lane = lanes_of((8, 128))

    def turn(value, shift):
        return pltpu.roll(value, shift % 128, 1) if shift % 128 else value

    if step_z:
        at_edge = lane % 16 == (0 if step_z == 1 else 15)
        moved = [
            {
                t: jnp.where(
                    at_edge,
                    turn(data[1 - k][t], 16 * step_y - 15 * step_z),
                    turn(data[k][t], 16 * step_y + step_z),
                )
                for t in need
            }
            for k in range(2)
        ]
    else:
        moved = [{t: turn(data[k][t], 16 * step_y) for t in need} for k in range(2)]
    if step_y:
        crossed = lane < 16 if step_y == 1 else lane >= 112
        moved = [
            {t: jnp.where(crossed, moved[k][(t - step_y) % 3], moved[k][t]) for t in tiles}
            for k in range(2)
        ]
    return moved


def advance(col, xg, yg, cp, tab, out, ext, nxt, ux, fs):
    me_x = lax.axis_index("bx")
    side = lax.rem(me_x, 2)
    mate = me_x + 1 - 2 * side

    def bit(table, device, k):
        row = tab[table]
        hit = (lanes_of(row.shape) == device) & (lax.broadcasted_iota(jnp.int32, row.shape, 0) == k)
        return jnp.sum(jnp.where(hit, row, 0).astype(F32))

    own_live = [bit(0, me_x, k) for k in range(2)]
    own_moving = [bit(1, me_x, k) for k in range(2)]
    arriving = [bit(1, mate, k) for k in range(2)]
    swap = (own_live[0] + own_live[1] < 0.5) & (arriving[0] + arriving[1] > 0.5)
    chosen = [
        jnp.where(swap, arriving[k], own_live[k] * (1.0 - own_moving[k])) > 0.5 for k in range(2)
    ]
    sc = jnp.where(swap, 1 - side, side)

    outer_near, outer_far = 7 + 17 * sc, 6 + 19 * sc
    inner_near, inner_far = 24 - 17 * sc, 25 - 19 * sc
    mate_near, mate_far = 15 * sc, 1 + 13 * sc
    lane8 = lanes_of((8, 128))

    def place_outer(k, tile, planes):
        ext[k, tile, pl.ds(outer_near, 19, stride=32), :] = planes[0:19, :]
        ext[k, tile, pl.ds((1 + sc) * 32 + outer_far, 1), :] = planes[19:20, :]
        ext[k, tile, pl.ds((7 + sc) * 32 + outer_far, 4, stride=64), :] = planes[20:24, :]

    for k in range(2):
        for tile in range(2):
            for q in range(19):
                ext[k, tile, q * 32 + 8 : q * 32 + 24, :] = col[sc, k, tile, q * 16 : q * 16 + 16, :]
            place_outer(k, tile, xg.at[sc, tile, k])
            ext[k, tile, pl.ds(inner_near, 19, stride=32), :] = col[
                1 - sc, k, tile, pl.ds(mate_near, 19, stride=16), :
            ]
            ext[k, tile, pl.ds(inner_far, 19, stride=32), :] = col[
                1 - sc, k, tile, pl.ds(mate_far, 19, stride=16), :
            ]
        for g in range(3):
            low = cp[0, sc, k]
            high = cp[1, sc, k]
            low = pltpu.roll(low, (96 - 32 * g) % 128, 1)
            high = pltpu.roll(high, (-32 * g) % 128, 1) if g else high
            ux[k, 8 * g : 8 * g + 8, :] = jnp.where(lane8 < 64, high, low)
        place_outer(k, 2, ux.at[k])

        for own in range(2):
            rows = 16 if own else 8
            lane = lanes_of((rows, 128))
            for q in range(19):
                parts = []
                for way in range(2):
                    near_lane, far_lane = ((112, 96), (0, 16))[way]

                    def unit(p, lane_to, way=way):
                        if own:
                            value = yg[way, sc, k, p // 8]
                        else:
                            value = yg[way, 1 - sc, k, p // 8, pl.ds(pl.multiple_of(8 * sc, 8), 8), :]
                        shift = (lane_to - 16 * (p % 8)) % 128
                        return pltpu.roll(value, shift, 1) if shift else value

                    value = unit(q, near_lane)
                    if q in RING_Y[way]:
                        far = unit(19 + RING_Y[way].index(q), far_lane)
                        value = jnp.where(lane // 16 == near_lane // 16, value, far)
                    parts.append(value)
                value = jnp.where(lane < 64, parts[1], parts[0])
                if own:
                    ext[k, 2, q * 32 + 8 : q * 32 + 24, :] = value
                else:
                    ext[k, 2, pl.ds(pl.multiple_of(q * 32 + 24 - 24 * sc, 8), 8), :] = value

    def arrive(source, stride, base, q, row, tiles):
        moved = stream(source, q, q * stride + base + row - VELOCITIES[q][0], tiles)
        result = {}
        for k in range(2):
            for t in tiles:
                value = moved[k][t]
                if q:
                    back = source[k, t, pl.ds(OPPOSITE[q] * stride + base + row, 8), :]
                    value = jnp.where(value > SOLID_TEST, value, back)
                result[k, t] = value
        return result

    for chunk in range(3):
        for q in range(19):
            for (k, t), value in arrive(ext, 32, 7, q, 8 * chunk, (0, 1, 2)).items():
                fs[q, k, t] = value
        for k in range(2):
            for t in range(3):
                f = [fs[q, k, t] for q in range(19)]
                fluid = f[0] > SOLID_TEST
                for q, value in enumerate(collide(f)):
                    nxt[k, t, q * 24 + 8 * chunk : q * 24 + 8 * chunk + 8, :] = jnp.where(
                        fluid, value, SOLID
                    )

    zero = jnp.zeros((8, 128), F32)
    both = chosen[0] & chosen[1]
    for chunk in range(2):
        for q in range(19):
            values = arrive(nxt, 24, 1, q, 8 * chunk, (0, 1))
            for t in range(2):
                spot = (q, slice(8 * chunk, 8 * chunk + 8), slice(128 * t, 128 * t + 128))
                lower, upper = values[0, t], values[1, t]
                out[(0,) + spot] = jnp.where(chosen[0], lower, jnp.where(chosen[1], upper, zero))
                out[(1,) + spot] = jnp.where(both, upper, zero)


VMEM = pl.BlockSpec(memory_space=pltpu.VMEM)
HBM = pl.BlockSpec(memory_space=pltpu.HBM)


def shards(n_x, n_y, populations, live_blocks, moving):
    pop, live, move = (
        pltpu.with_memory_space_constraint(array, pltpu.HBM)
        for array in (
            populations.reshape(2, 19, 16, 256),
            jnp.transpose(live_blocks, (1, 2, 0)),
            jnp.transpose(moving, (1, 2, 0)),
        )
    )
    shapes = [(2, 2, 2, 304, 128), (2, 2, 2, 24, 128), (2, 2, 2, 3, 16, 128), (2, 2, 2, 8, 128)]
    parts = pl.pallas_call(
        functools.partial(exchange, n_x, n_y),
        out_shape=[jax.ShapeDtypeStruct(shape, F32) for shape in shapes]
        + [jax.ShapeDtypeStruct((2, 2, n_x), jnp.int32)],
        in_specs=[HBM] * 3,
        out_specs=[VMEM] * 5,
        scratch_shapes=[
            pltpu.VMEM((2, 2, 19, 16, 256), F32),
            pltpu.VMEM((2, 2, 2, 24, 128), F32),
            pltpu.VMEM((2, 2, 2, 3, 16, 128), F32),
            pltpu.VMEM((2, 2, 2, 8, 128), F32),
            pltpu.SemaphoreType.DMA((3,)),
            pltpu.SemaphoreType.DMA((16,)),
            pltpu.SemaphoreType.DMA((16,)),
            pltpu.SemaphoreType.REGULAR,
        ],
        compiler_params=pltpu.CompilerParams(
            collective_id=0, has_side_effects=True, vmem_limit_bytes=8 << 20
        ),
        name="exchange",
    )(pop, live, move)
    result = pl.pallas_call(
        advance,
        out_shape=jax.ShapeDtypeStruct((2, 19, 16, 256), F32),
        in_specs=[VMEM] * 5,
        out_specs=VMEM,
        scratch_shapes=[
            pltpu.VMEM((2, 3, 19 * 32, 128), F32),
            pltpu.VMEM((2, 3, 19 * 24, 128), F32),
            pltpu.VMEM((2, 24, 128), F32),
            pltpu.VMEM((19, 2, 3, 8, 128), F32),
        ],
        compiler_params=pltpu.CompilerParams(vmem_limit_bytes=12 << 20),
        name="advance",
    )(*parts)
    return result.reshape(1, 1, 2, 19, 16, 256)


def solution(mesh):
    n_x, n_y = mesh.shape["bx"], mesh.shape["by"]
    placed = (P("bx", "by", None, None, None, None), P(), P())
    return jax.shard_map(
        functools.partial(shards, n_x, n_y),
        mesh=mesh,
        in_specs=placed,
        out_specs=P("bx", "by", None, None, None, None),
        check_vma=False,
    )
```

```python
import functools

import jax
import jax.numpy as jnp
from jax import lax
from jax.experimental import pallas as pl
from jax.experimental.pallas import tpu as pltpu
from jax.sharding import PartitionSpec as P

MESH = pl.DeviceIdType.MESH
VELOCITIES = [
    (0, 0, 0), (1, 0, 0), (-1, 0, 0), (0, 1, 0), (0, -1, 0), (0, 0, 1), (0, 0, -1),
    (1, 1, 0), (-1, -1, 0), (1, -1, 0), (-1, 1, 0), (1, 0, 1), (-1, 0, -1),
    (1, 0, -1), (-1, 0, 1), (0, 1, 1), (0, -1, -1), (0, 1, -1), (0, -1, 1),
]
OPPOSITE = [0, 2, 1, 4, 3, 6, 5, 8, 7, 10, 9, 12, 11, 14, 13, 16, 15, 18, 17]
SMAG_COEF = 18.0 * 2.0**0.5 * 0.17**2
SOLID = -1e30
SOLID_TEST = -1e29
RING_Y = ([3, 7, 10, 15, 17], [4, 8, 9, 16, 18])
F32 = jnp.float32


def collide(f):
    sums, diffs = {}, {}
    for i in range(1, 19, 2):
        sums[i] = f[i] + f[i + 1]
        diffs[i] = f[i] - f[i + 1]
    side_xy = sums[7] + sums[9]
    side_xz = sums[11] + sums[13]
    side_yz = sums[15] + sums[17]
    density = f[0] + (sums[1] + sums[3] + sums[5]) + (side_xy + side_xz + side_yz)
    mom_x = diffs[1] + (diffs[7] + diffs[9]) + (diffs[11] + diffs[13])
    mom_y = diffs[3] + (diffs[7] - diffs[9]) + (diffs[15] + diffs[17])
    mom_z = diffs[5] + (diffs[11] - diffs[13]) + (diffs[15] - diffs[17])
    inverse = 1.0 / density
    vel_x, vel_y, vel_z = mom_x * inverse, mom_y * inverse, mom_z * inverse
    third = density * (1.0 / 3.0)
    p_xx = sums[1] + side_xy + side_xz - third - mom_x * vel_x
    p_yy = sums[3] + side_xy + side_yz - third - mom_y * vel_y
    p_zz = sums[5] + side_xz + side_yz - third - mom_z * vel_z
    p_xy = sums[7] - sums[9] - mom_x * vel_y
    p_xz = sums[11] - sums[13] - mom_x * vel_z
    p_yz = sums[15] - sums[17] - mom_y * vel_z
    strength = jnp.sqrt(
        p_xx * p_xx + p_yy * p_yy + p_zz * p_zz + 2.0 * (p_xy * p_xy + p_xz * p_xz + p_yz * p_yz)
    )
    omega = 2.0 / (0.6 + jnp.sqrt(0.36 + SMAG_COEF * strength * inverse))
    keep = 1.0 - omega
    gain = omega * density
    speed = vel_x * vel_x + vel_y * vel_y + vel_z * vel_z
    base = 1.0 - 1.5 * speed
    edge, corner = gain * (1.0 / 18.0), gain * (1.0 / 36.0)
    base_edge, base_corner = edge * base, corner * base
    result = [None] * 19
    result[0] = f[0] * keep + (gain * (1.0 / 3.0)) * base
    along = {
        1: vel_x, 3: vel_y, 5: vel_z,
        7: vel_x + vel_y, 9: vel_x - vel_y, 11: vel_x + vel_z,
        13: vel_x - vel_z, 15: vel_y + vel_z, 17: vel_y - vel_z,
    }
    for i in range(1, 19, 2):
        weight, rest = (edge, base_edge) if i < 7 else (corner, base_corner)
        odd = 3.0 * weight * along[i]
        even = rest + (1.5 * odd) * along[i]
        result[i] = f[i] * keep + (even + odd)
        result[i + 1] = f[i + 1] * keep + (even - odd)
    return result


def lanes_of(shape):
    return lax.broadcasted_iota(jnp.int32, shape, len(shape) - 1)


def exchange(
    n_x, n_y, pop, live, move, ext, tab,
    col, xg, yg, cp, fbuf, xs, ys, cs, ux, in_sem, send_sem, recv_sem, allowed,
):
    me_x, me_y = lax.axis_index("bx"), lax.axis_index("by")
    side = lax.rem(me_x, 2)
    base = me_x - side
    hub = base + 1
    at_mate = (base + 1 - side, me_y)
    prev_hub = lax.rem(base + n_x - 1, n_x)
    next_hub = lax.rem(base + 3, n_x)
    next_zero = lax.rem(base + 2, n_x)
    rows_y = (lax.rem(me_y + 1, n_y), lax.rem(me_y + n_y - 1, n_y))
    barrier = pltpu.get_barrier_semaphore()

    def greet(semaphore, devices):
        for device in devices:
            pl.semaphore_signal(semaphore, inc=1, device_id=device, device_id_type=MESH)

    @pl.when(side == 1)
    def _():
        around = (me_y,) + rows_y
        greet(barrier, [(prev_hub, y) for y in around] + [(hub, y) for y in rows_y] + [(next_zero, y) for y in around])

    @pl.when(side == 0)
    def _():
        greet(barrier, [at_mate])

    load_pop = pltpu.make_async_copy(pop, fbuf.at[side], in_sem.at[0])
    load_live = pltpu.make_async_copy(live.at[me_y], tab.at[0], in_sem.at[1])
    load_move = pltpu.make_async_copy(move.at[me_y], tab.at[1], in_sem.at[2])
    load_pop.start()
    load_live.start()
    load_move.start()

    def link(index, source, target, device):
        return pltpu.make_async_remote_copy(
            src_ref=source,
            dst_ref=target,
            send_sem=send_sem.at[index],
            recv_sem=recv_sem.at[index],
            device_id=device,
            device_id_type=MESH,
        )

    raw = link(0, pop, fbuf.at[side], at_mate)
    high = link(1, xs.at[1], xg.at[0], (next_hub, me_y))
    low = link(2, xs.at[0], xg.at[1], (prev_hub, me_y))
    high_corner = [link(3 + w, cs.at[w, 1], cp.at[w, 0], (next_hub, rows_y[w])) for w in range(2)]
    low_corner = [link(5 + w, cs.at[w, 0], cp.at[w, 1], (prev_hub, rows_y[w])) for w in range(2)]
    face = [
        [link(7 + 2 * w + c, ys.at[w, c], yg.at[w, c], (hub, rows_y[w])) for w in range(2)] for c in range(2)
    ]
    relay_x = link(11, xg, xg, at_mate)
    relay_y = [link(12 + w, yg.at[w], yg.at[w], at_mate) for w in range(2)]
    relay_c = [link(14 + w, cp.at[w], cp.at[w], at_mate) for w in range(2)]

    load_live.wait()
    load_move.wait()
    load_pop.wait()

    def relax_column(c):
        row = tab[0]
        hit = lanes_of(row.shape) == base + c
        flags = jnp.sum(jnp.where(hit, row, 0).astype(F32), axis=1, keepdims=True)
        first = jnp.broadcast_to(flags[0:1, :], (8, 128)) > 0.5
        second = jnp.broadcast_to(flags[1:2, :], (8, 128)) > 0.5
        for k in range(2):
            fluid = (first, second)[k]

            def relax(i, carry, k=k, fluid=fluid):
                tile, half = i // 2, i % 2
                rows = pl.ds(pl.multiple_of(half * 8, 8), 8)
                lanes = pl.ds(pl.multiple_of(tile * 128, 128), 128)
                f = [
                    jnp.where(first, fbuf[c, k, q, rows, lanes], fbuf[c, 1 - k, q, rows, lanes])
                    for q in range(19)
                ]
                for q, value in enumerate(collide(f)):
                    to = pl.ds(pl.multiple_of(q * 16 + half * 8, 8), 8)
                    col[c, k, tile, to, :] = jnp.where(fluid, value, SOLID)
                return carry

            lax.fori_loop(0, 4, relax, 0)

    group = lanes_of((16, 128)) // 16
    quarter = lanes_of((8, 128)) // 32

    def pack_x(c):
        near, far = 15 * c, 1 + 13 * c
        for tile in range(2):
            for k in range(2):
                own = col.at[c, k, tile]
                xs[c, tile, k, 0:19, :] = own[pl.ds(near, 19, stride=16), :]
                xs[c, tile, k, 19:20, :] = own[pl.ds((2 - c) * 16 + far, 1), :]
                xs[c, tile, k, 20:24, :] = own[pl.ds((8 - c) * 16 + far, 4, stride=32), :]
        for way in range(2):
            for k in range(2):
                packed = None
                for g in range(3):
                    value = xs[c, 1 - way, k, 8 * g : 8 * g + 8, :]
                    shift = (32 * g - (96, 0)[way]) % 128
                    if shift:
                        value = pltpu.roll(value, shift, 1)
                    packed = value if packed is None else jnp.where(quarter == g, value, packed)
                cs[way, c, k] = packed

    def pack_y(c):
        def pack(k, carry):
            for way in range(2):
                tile, first_lane, second_lane = ((1, 112, 96), (0, 0, 16))[way]
                for g in range(3):
                    packed = None
                    for i in range(8):
                        p = 8 * g + i
                        q, lane = (p, first_lane) if p < 19 else (RING_Y[way][p - 19], second_lane)
                        value = col[c, k, tile, q * 16 : q * 16 + 16, :]
                        shift = (16 * i - lane) % 128
                        if shift:
                            value = pltpu.roll(value, shift, 1)
                        packed = value if packed is None else jnp.where(group == i, value, packed)
                    ys[way, c, k, g] = packed
            return carry

        lax.fori_loop(0, 2, pack, 0)

    relax_column(side)

    @pl.when(side == 1)
    def _():
        pack_x(1)
        pl.semaphore_wait(barrier, 6)
        greet(allowed, [at_mate])
        for copy in high_corner + [high]:
            copy.start()
        pack_y(1)
        for copy in face[1] + [raw]:
            copy.start()

    @pl.when(side == 0)
    def _():
        pack_x(0)
        pack_y(0)
        pl.semaphore_wait(allowed, 1)
        for copy in face[0] + [raw]:
            copy.start()
        pl.semaphore_wait(barrier, 3)
        for copy in low_corner + [low]:
            copy.start()

    raw.wait_recv()
    relax_column(1 - side)

    def pair(table, device):
        row = tab[table]
        one = jnp.sum(jnp.where(lanes_of(row.shape) == device, row, 0).astype(F32), axis=1, keepdims=True)
        return one[0:1, :] + one[1:2, :]

    swap = jnp.where(pair(0, me_x) < 0.5, jnp.where(pair(1, base + 1 - side) > 0.5, 1.0, 0.0), 0.0)
    column = jnp.abs(swap - side.astype(F32))

    def first_or_second(first, second):
        return jnp.where(jnp.broadcast_to(column, first.shape) < 0.5, first, second)

    def every(start, count=19, stride=32):
        return pl.ds(start, count, stride=stride)

    def gather_columns(k, carry):
        for tile in range(2):
            for q in range(19):
                rows = slice(q * 16, q * 16 + 16)
                ext[k, tile, q * 32 + 8 : q * 32 + 24, :] = first_or_second(
                    col[0, k, tile, rows, :], col[1, k, tile, rows, :]
                )
        return carry

    lax.fori_loop(0, 2, gather_columns, 0)

    @pl.when(side == 1)
    def _():
        high.wait_recv()
        low.wait_recv()
        relay_x.start()

    @pl.when(side == 0)
    def _():
        relay_x.wait_recv()

    def place_ghost(k, tile, c, planes, inner_near, inner_far):
        near, far = ((7, 6), (24, 25))[c]

        def choose(outer, inner):
            return first_or_second(outer, inner) if c == 0 else first_or_second(inner, outer)

        ext[k, tile, every(near), :] = choose(planes[0:19, :], inner_near)
        ext[k, tile, every(far), :] = inner_far
        one = pl.ds((1 + c) * 32 + far, 1)
        ext[k, tile, one, :] = choose(planes[19:20, :], ext[k, tile, one, :])
        four = every((7 + c) * 32 + far, 4, 64)
        ext[k, tile, four, :] = choose(planes[20:24, :], ext[k, tile, four, :])

    def gather_x(k, carry):
        for tile in range(2):
            for c in range(2):
                near, far = ((15, 14), (0, 1))[c]
                place_ghost(
                    k, tile, c, xg.at[c, tile, k],
                    col[c, k, tile, every(near, stride=16), :], col[c, k, tile, every(far, stride=16), :],
                )
        return carry

    lax.fori_loop(0, 2, gather_x, 0)

    @pl.when(side == 1)
    def _():
        for w in range(2):
            face[1][w].wait_recv()
            face[0][w].wait_recv()
            relay_y[w].start()

    @pl.when(side == 0)
    def _():
        for copy in relay_y:
            copy.wait_recv()

    def unpack(units, q, rows):
        lane = lanes_of((rows, 128))
        parts = []
        for way in range(2):
            near_lane, far_lane = ((112, 96), (0, 16))[way]

            def unit(p, lane_to, way=way):
                shift = (lane_to - 16 * (p % 8)) % 128
                value = units[way][p // 8]
                return pltpu.roll(value, shift, 1) if shift else value

            value = unit(q, near_lane)
            if q in RING_Y[way]:
                far = unit(19 + RING_Y[way].index(q), far_lane)
                value = jnp.where(lane // 16 == near_lane // 16, value, far)
            parts.append(value)
        return jnp.where(lane < 64, parts[1], parts[0])

    def gather_y(k, carry):
        units = [[first_or_second(yg[w, 0, k, g], yg[w, 1, k, g]) for g in range(3)] for w in range(2)]
        for q in range(19):
            ext[k, 2, q * 32 + 8 : q * 32 + 24, :] = unpack(units, q, 16)
        for c in range(2):
            rows = (slice(8, 16), slice(0, 8))[c]
            units = [[yg[w, c, k, g, rows, :] for g in range(3)] for w in range(2)]
            for q in range(19):
                start = q * 32 + 24 * c
                ext[k, 2, start : start + 8, :] = unpack(units, q, 8)
        return carry

    lax.fori_loop(0, 2, gather_y, 0)

    @pl.when(side == 1)
    def _():
        for w in range(2):
            high_corner[w].wait_recv()
            low_corner[w].wait_recv()
            relay_c[w].start()

    @pl.when(side == 0)
    def _():
        for copy in relay_c:
            copy.wait_recv()

    lane8 = lanes_of((8, 128))
    for k in range(2):
        for c in range(2):
            for g in range(3):
                up = pltpu.roll(cp[0, c, k], (96 - 32 * g) % 128, 1)
                down = cp[1, c, k]
                down = pltpu.roll(down, (-32 * g) % 128, 1) if g else down
                ux[k, c, 8 * g : 8 * g + 8, :] = jnp.where(lane8 < 64, down, up)
            near, far = ((7, 6), (24, 25))[c]
            place_ghost(k, 2, c, ux.at[k, c], ext[k, 2, every(near), :], ext[k, 2, every(far), :])

    @pl.when(side == 1)
    def _():
        for copy in high_corner + face[1] + [high, relay_x] + relay_y + relay_c:
            copy.wait_send()

    @pl.when(side == 0)
    def _():
        for copy in low_corner + face[0] + [low]:
            copy.wait_send()

    raw.wait_send()


def stream(source, q, row, tiles):
    _, step_y, step_z = VELOCITIES[q]
    need = sorted({(t - d) % 3 for t in tiles for d in ((0, step_y) if step_y else (0,))})
    data = [{t: source[k, t, pl.ds(row, 8), :] for t in need} for k in range(2)]
    lane = lanes_of((8, 128))

    def turn(value, shift):
        return pltpu.roll(value, shift % 128, 1) if shift % 128 else value

    if step_z:
        at_edge = lane % 16 == (0 if step_z == 1 else 15)
        moved = [
            {
                t: jnp.where(
                    at_edge,
                    turn(data[1 - k][t], 16 * step_y - 15 * step_z),
                    turn(data[k][t], 16 * step_y + step_z),
                )
                for t in need
            }
            for k in range(2)
        ]
    else:
        moved = [{t: turn(data[k][t], 16 * step_y) for t in need} for k in range(2)]
    if step_y:
        crossed = lane < 16 if step_y == 1 else lane >= 112
        moved = [
            {t: jnp.where(crossed, moved[k][(t - step_y) % 3], moved[k][t]) for t in tiles}
            for k in range(2)
        ]
    return moved


def advance(ext, tab, out, nxt, fs):
    me_x = lax.axis_index("bx")
    side = lax.rem(me_x, 2)
    mate = me_x + 1 - 2 * side

    def bit(table, device, k):
        row = tab[table]
        hit = (lanes_of(row.shape) == device) & (lax.broadcasted_iota(jnp.int32, row.shape, 0) == k)
        return jnp.sum(jnp.where(hit, row, 0).astype(F32))

    own_live = [bit(0, me_x, k) for k in range(2)]
    own_moving = [bit(1, me_x, k) for k in range(2)]
    arriving = [bit(1, mate, k) for k in range(2)]
    swap = (own_live[0] + own_live[1] < 0.5) & (arriving[0] + arriving[1] > 0.5)
    chosen = [
        jnp.where(swap, arriving[k], own_live[k] * (1.0 - own_moving[k])) > 0.5 for k in range(2)
    ]

    def arrive(source, stride, base, q, row, tiles):
        moved = stream(source, q, q * stride + base + row - VELOCITIES[q][0], tiles)
        result = {}
        for k in range(2):
            for t in tiles:
                value = moved[k][t]
                if q:
                    back = source[k, t, pl.ds(OPPOSITE[q] * stride + base + row, 8), :]
                    value = jnp.where(value > SOLID_TEST, value, back)
                result[k, t] = value
        return result

    for chunk in range(3):
        for q in range(19):
            for (k, t), value in arrive(ext, 32, 7, q, 8 * chunk, (0, 1, 2)).items():
                fs[q, k, t] = value
        for k in range(2):
            for t in range(3):
                f = [fs[q, k, t] for q in range(19)]
                fluid = f[0] > SOLID_TEST
                for q, value in enumerate(collide(f)):
                    nxt[k, t, q * 24 + 8 * chunk : q * 24 + 8 * chunk + 8, :] = jnp.where(
                        fluid, value, SOLID
                    )

    zero = jnp.zeros((8, 128), F32)
    both = chosen[0] & chosen[1]
    for chunk in range(2):
        for q in range(19):
            values = arrive(nxt, 24, 1, q, 8 * chunk, (0, 1))
            for t in range(2):
                spot = (q, slice(8 * chunk, 8 * chunk + 8), slice(128 * t, 128 * t + 128))
                lower, upper = values[0, t], values[1, t]
                out[(0,) + spot] = jnp.where(chosen[0], lower, jnp.where(chosen[1], upper, zero))
                out[(1,) + spot] = jnp.where(both, upper, zero)


VMEM = pl.BlockSpec(memory_space=pltpu.VMEM)
HBM = pl.BlockSpec(memory_space=pltpu.HBM)


def shards(n_x, n_y, populations, live_blocks, moving):
    pop, live, move = (
        pltpu.with_memory_space_constraint(array, pltpu.HBM)
        for array in (
            populations.reshape(2, 19, 16, 256),
            jnp.transpose(live_blocks, (1, 2, 0)),
            jnp.transpose(moving, (1, 2, 0)),
        )
    )
    parts = pl.pallas_call(
        functools.partial(exchange, n_x, n_y),
        out_shape=[
            jax.ShapeDtypeStruct((2, 3, 19 * 32, 128), F32),
            jax.ShapeDtypeStruct((2, 2, n_x), jnp.int32),
        ],
        in_specs=[HBM] * 3,
        out_specs=[VMEM] * 2,
        scratch_shapes=[
            pltpu.VMEM((2, 2, 2, 304, 128), F32),
            pltpu.VMEM((2, 2, 2, 24, 128), F32),
            pltpu.VMEM((2, 2, 2, 3, 16, 128), F32),
            pltpu.VMEM((2, 2, 2, 8, 128), F32),
            pltpu.VMEM((2, 2, 19, 16, 256), F32),
            pltpu.VMEM((2, 2, 2, 24, 128), F32),
            pltpu.VMEM((2, 2, 2, 3, 16, 128), F32),
            pltpu.VMEM((2, 2, 2, 8, 128), F32),
            pltpu.VMEM((2, 2, 24, 128), F32),
            pltpu.SemaphoreType.DMA((3,)),
            pltpu.SemaphoreType.DMA((16,)),
            pltpu.SemaphoreType.DMA((16,)),
            pltpu.SemaphoreType.REGULAR,
        ],
        compiler_params=pltpu.CompilerParams(
            collective_id=0, has_side_effects=True, vmem_limit_bytes=12 << 20
        ),
        name="exchange",
    )(pop, live, move)
    result = pl.pallas_call(
        advance,
        out_shape=jax.ShapeDtypeStruct((2, 19, 16, 256), F32),
        in_specs=[VMEM] * 2,
        out_specs=VMEM,
        scratch_shapes=[
            pltpu.VMEM((2, 3, 19 * 24, 128), F32),
            pltpu.VMEM((19, 2, 3, 8, 128), F32),
        ],
        compiler_params=pltpu.CompilerParams(vmem_limit_bytes=12 << 20),
        name="advance",
    )(*parts)
    return result.reshape(1, 1, 2, 19, 16, 256)


def solution(mesh):
    n_x, n_y = mesh.shape["bx"], mesh.shape["by"]
    placed = (P("bx", "by", None, None, None, None), P(), P())
    return jax.shard_map(
        functools.partial(shards, n_x, n_y),
        mesh=mesh,
        in_specs=placed,
        out_specs=P("bx", "by", None, None, None, None),
        check_vma=False,
    )
```

```python
import functools

import jax
import jax.numpy as jnp
from jax import lax
from jax.experimental import pallas as pl
from jax.experimental.pallas import tpu as pltpu
from jax.sharding import PartitionSpec as P

MESH = pl.DeviceIdType.MESH
VELOCITIES = [
    (0, 0, 0), (1, 0, 0), (-1, 0, 0), (0, 1, 0), (0, -1, 0), (0, 0, 1), (0, 0, -1),
    (1, 1, 0), (-1, -1, 0), (1, -1, 0), (-1, 1, 0), (1, 0, 1), (-1, 0, -1),
    (1, 0, -1), (-1, 0, 1), (0, 1, 1), (0, -1, -1), (0, 1, -1), (0, -1, 1),
]
OPPOSITE = [0, 2, 1, 4, 3, 6, 5, 8, 7, 10, 9, 12, 11, 14, 13, 16, 15, 18, 17]
SMAG_COEF = 18.0 * 2.0**0.5 * 0.17**2
SOLID = -1e30
SOLID_TEST = -1e29
RING_Y = ([3, 7, 10, 15, 17], [4, 8, 9, 16, 18])
F32 = jnp.float32


def collide(f):
    sums, diffs = {}, {}
    for i in range(1, 19, 2):
        sums[i] = f[i] + f[i + 1]
        diffs[i] = f[i] - f[i + 1]
    side_xy = sums[7] + sums[9]
    side_xz = sums[11] + sums[13]
    side_yz = sums[15] + sums[17]
    density = f[0] + (sums[1] + sums[3] + sums[5]) + (side_xy + side_xz + side_yz)
    mom_x = diffs[1] + (diffs[7] + diffs[9]) + (diffs[11] + diffs[13])
    mom_y = diffs[3] + (diffs[7] - diffs[9]) + (diffs[15] + diffs[17])
    mom_z = diffs[5] + (diffs[11] - diffs[13]) + (diffs[15] - diffs[17])
    inverse = 1.0 / density
    vel_x, vel_y, vel_z = mom_x * inverse, mom_y * inverse, mom_z * inverse
    third = density * (1.0 / 3.0)
    p_xx = sums[1] + side_xy + side_xz - third - mom_x * vel_x
    p_yy = sums[3] + side_xy + side_yz - third - mom_y * vel_y
    p_zz = sums[5] + side_xz + side_yz - third - mom_z * vel_z
    p_xy = sums[7] - sums[9] - mom_x * vel_y
    p_xz = sums[11] - sums[13] - mom_x * vel_z
    p_yz = sums[15] - sums[17] - mom_y * vel_z
    strength = jnp.sqrt(
        p_xx * p_xx + p_yy * p_yy + p_zz * p_zz + 2.0 * (p_xy * p_xy + p_xz * p_xz + p_yz * p_yz)
    )
    omega = 2.0 / (0.6 + jnp.sqrt(0.36 + SMAG_COEF * strength * inverse))
    keep = 1.0 - omega
    gain = omega * density
    speed = vel_x * vel_x + vel_y * vel_y + vel_z * vel_z
    base = 1.0 - 1.5 * speed
    edge, corner = gain * (1.0 / 18.0), gain * (1.0 / 36.0)
    base_edge, base_corner = edge * base, corner * base
    result = [None] * 19
    result[0] = f[0] * keep + (gain * (1.0 / 3.0)) * base
    along = {
        1: vel_x, 3: vel_y, 5: vel_z,
        7: vel_x + vel_y, 9: vel_x - vel_y, 11: vel_x + vel_z,
        13: vel_x - vel_z, 15: vel_y + vel_z, 17: vel_y - vel_z,
    }
    for i in range(1, 19, 2):
        weight, rest = (edge, base_edge) if i < 7 else (corner, base_corner)
        odd = 3.0 * weight * along[i]
        even = rest + (1.5 * odd) * along[i]
        result[i] = f[i] * keep + (even + odd)
        result[i + 1] = f[i + 1] * keep + (even - odd)
    return result


def lanes_of(shape):
    return lax.broadcasted_iota(jnp.int32, shape, len(shape) - 1)


def exchange(
    n_x, n_y, pop, live, move, ext, tab,
    col, xg, yg, cp, fbuf, xs, ys, cs, ux, in_sem, send_sem, recv_sem, allowed,
):
    me_x, me_y = lax.axis_index("bx"), lax.axis_index("by")
    side = lax.rem(me_x, 2)
    base = me_x - side
    hub = base + 1
    at_mate = (base + 1 - side, me_y)
    prev_hub = lax.rem(base + n_x - 1, n_x)
    next_hub = lax.rem(base + 3, n_x)
    next_zero = lax.rem(base + 2, n_x)
    rows_y = (lax.rem(me_y + 1, n_y), lax.rem(me_y + n_y - 1, n_y))
    barrier = pltpu.get_barrier_semaphore()

    def greet(semaphore, devices):
        for device in devices:
            pl.semaphore_signal(semaphore, inc=1, device_id=device, device_id_type=MESH)

    @pl.when(side == 1)
    def _():
        around = (me_y,) + rows_y
        greet(barrier, [(prev_hub, y) for y in around] + [(hub, y) for y in rows_y] + [(next_zero, y) for y in around])

    @pl.when(side == 0)
    def _():
        greet(barrier, [at_mate])

    load_pop = pltpu.make_async_copy(pop, fbuf.at[side], in_sem.at[0])
    load_live = pltpu.make_async_copy(live.at[me_y], tab.at[0], in_sem.at[1])
    load_move = pltpu.make_async_copy(move.at[me_y], tab.at[1], in_sem.at[2])
    load_pop.start()
    load_live.start()
    load_move.start()

    def link(index, source, target, device):
        return pltpu.make_async_remote_copy(
            src_ref=source,
            dst_ref=target,
            send_sem=send_sem.at[index],
            recv_sem=recv_sem.at[index],
            device_id=device,
            device_id_type=MESH,
        )

    raw = link(0, pop, fbuf.at[side], at_mate)
    high = link(1, xs.at[1], xg.at[0], (next_hub, me_y))
    low = link(2, xs.at[0], xg.at[1], (prev_hub, me_y))
    high_corner = [link(3 + w, cs.at[w, 1], cp.at[w, 0], (next_hub, rows_y[w])) for w in range(2)]
    low_corner = [link(5 + w, cs.at[w, 0], cp.at[w, 1], (prev_hub, rows_y[w])) for w in range(2)]
    face = [
        [link(7 + 2 * w + c, ys.at[w, c], yg.at[w, c], (hub, rows_y[w])) for w in range(2)] for c in range(2)
    ]
    relay_x = link(11, xg, xg, at_mate)
    relay_y = [link(12 + w, yg.at[w], yg.at[w], at_mate) for w in range(2)]
    relay_c = [link(14 + w, cp.at[w], cp.at[w], at_mate) for w in range(2)]

    load_live.wait()
    load_move.wait()
    load_pop.wait()

    def relax_column(c):
        row = tab[0]
        hit = lanes_of(row.shape) == base + c
        flags = jnp.sum(jnp.where(hit, row, 0).astype(F32), axis=1, keepdims=True)
        first = jnp.broadcast_to(flags[0:1, :], (8, 128)) > 0.5
        second = jnp.broadcast_to(flags[1:2, :], (8, 128)) > 0.5
        for k in range(2):
            fluid = (first, second)[k]

            def relax(i, carry, k=k, fluid=fluid):
                tile, half = i // 2, i % 2
                rows = pl.ds(pl.multiple_of(half * 8, 8), 8)
                lanes = pl.ds(pl.multiple_of(tile * 128, 128), 128)
                f = [
                    jnp.where(first, fbuf[c, k, q, rows, lanes], fbuf[c, 1 - k, q, rows, lanes])
                    for q in range(19)
                ]
                for q, value in enumerate(collide(f)):
                    to = pl.ds(pl.multiple_of(q * 16 + half * 8, 8), 8)
                    col[c, k, tile, to, :] = jnp.where(fluid, value, SOLID)
                return carry

            lax.fori_loop(0, 4, relax, 0)

    group = lanes_of((16, 128)) // 16
    quarter = lanes_of((8, 128)) // 32

    def pack_x(c):
        near, far = 15 * c, 1 + 13 * c
        for tile in range(2):
            for k in range(2):
                own = col.at[c, k, tile]
                xs[c, tile, k, 0:19, :] = own[pl.ds(near, 19, stride=16), :]
                xs[c, tile, k, 19:20, :] = own[pl.ds((2 - c) * 16 + far, 1), :]
                xs[c, tile, k, 20:24, :] = own[pl.ds((8 - c) * 16 + far, 4, stride=32), :]
        for way in range(2):
            for k in range(2):
                packed = None
                for g in range(3):
                    value = xs[c, 1 - way, k, 8 * g : 8 * g + 8, :]
                    shift = (32 * g - (96, 0)[way]) % 128
                    if shift:
                        value = pltpu.roll(value, shift, 1)
                    packed = value if packed is None else jnp.where(quarter == g, value, packed)
                cs[way, c, k] = packed

    def pack_y(c):
        def pack(k, carry):
            for way in range(2):
                tile, first_lane, second_lane = ((1, 112, 96), (0, 0, 16))[way]
                for g in range(3):
                    packed = None
                    for i in range(8):
                        p = 8 * g + i
                        q, lane = (p, first_lane) if p < 19 else (RING_Y[way][p - 19], second_lane)
                        value = col[c, k, tile, q * 16 : q * 16 + 16, :]
                        shift = (16 * i - lane) % 128
                        if shift:
                            value = pltpu.roll(value, shift, 1)
                        packed = value if packed is None else jnp.where(group == i, value, packed)
                    ys[way, c, k, g] = packed
            return carry

        lax.fori_loop(0, 2, pack, 0)

    relax_column(side)

    @pl.when(side == 1)
    def _():
        pack_x(1)
        pl.semaphore_wait(barrier, 6)
        greet(allowed, [at_mate])
        for copy in high_corner + [high]:
            copy.start()
        pack_y(1)
        for copy in face[1] + [raw]:
            copy.start()

    @pl.when(side == 0)
    def _():
        pack_x(0)
        pack_y(0)
        pl.semaphore_wait(allowed, 1)
        for copy in face[0] + [raw]:
            copy.start()
        pl.semaphore_wait(barrier, 3)
        for copy in low_corner + [low]:
            copy.start()

    raw.wait_recv()
    relax_column(1 - side)

    def pair(table, device):
        row = tab[table]
        one = jnp.sum(jnp.where(lanes_of(row.shape) == device, row, 0).astype(F32), axis=1, keepdims=True)
        return one[0:1, :] + one[1:2, :]

    swap = jnp.where(pair(0, me_x) < 0.5, jnp.where(pair(1, base + 1 - side) > 0.5, 1.0, 0.0), 0.0)
    column = jnp.abs(swap - side.astype(F32))

    def first_or_second(first, second):
        return jnp.where(jnp.broadcast_to(column, first.shape) < 0.5, first, second)

    def every(start, count=19, stride=32):
        return pl.ds(start, count, stride=stride)

    def gather_columns(k, carry):
        for tile in range(2):
            for q in range(19):
                rows = slice(q * 16, q * 16 + 16)
                ext[k, tile, q * 32 + 8 : q * 32 + 24, :] = first_or_second(
                    col[0, k, tile, rows, :], col[1, k, tile, rows, :]
                )
        return carry

    lax.fori_loop(0, 2, gather_columns, 0)

    @pl.when(side == 1)
    def _():
        for w in range(2):
            face[1][w].wait_recv()
            face[0][w].wait_recv()
            relay_y[w].start()

    @pl.when(side == 0)
    def _():
        for copy in relay_y:
            copy.wait_recv()

    def unpack(units, q, rows):
        lane = lanes_of((rows, 128))
        parts = []
        for way in range(2):
            near_lane, far_lane = ((112, 96), (0, 16))[way]

            def unit(p, lane_to, way=way):
                shift = (lane_to - 16 * (p % 8)) % 128
                value = units[way][p // 8]
                return pltpu.roll(value, shift, 1) if shift else value

            value = unit(q, near_lane)
            if q in RING_Y[way]:
                far = unit(19 + RING_Y[way].index(q), far_lane)
                value = jnp.where(lane // 16 == near_lane // 16, value, far)
            parts.append(value)
        return jnp.where(lane < 64, parts[1], parts[0])

    def gather_y(k, carry):
        units = [[first_or_second(yg[w, 0, k, g], yg[w, 1, k, g]) for g in range(3)] for w in range(2)]
        for q in range(19):
            ext[k, 2, q * 32 + 8 : q * 32 + 24, :] = unpack(units, q, 16)
        for c in range(2):
            rows = (slice(8, 16), slice(0, 8))[c]
            units = [[yg[w, c, k, g, rows, :] for g in range(3)] for w in range(2)]
            for q in range(19):
                start = q * 32 + 24 * c
                ext[k, 2, start : start + 8, :] = unpack(units, q, 8)
        return carry

    lax.fori_loop(0, 2, gather_y, 0)

    @pl.when(side == 1)
    def _():
        high.wait_recv()
        low.wait_recv()
        relay_x.start()

    @pl.when(side == 0)
    def _():
        relay_x.wait_recv()

    def place_ghost(k, tile, c, planes, inner_near, inner_far):
        near, far = ((7, 6), (24, 25))[c]

        def choose(outer, inner):
            return first_or_second(outer, inner) if c == 0 else first_or_second(inner, outer)

        ext[k, tile, every(near), :] = choose(planes[0:19, :], inner_near)
        ext[k, tile, every(far), :] = inner_far
        one = pl.ds((1 + c) * 32 + far, 1)
        ext[k, tile, one, :] = choose(planes[19:20, :], ext[k, tile, one, :])
        four = every((7 + c) * 32 + far, 4, 64)
        ext[k, tile, four, :] = choose(planes[20:24, :], ext[k, tile, four, :])

    def gather_x(k, carry):
        for tile in range(2):
            for c in range(2):
                near, far = ((15, 14), (0, 1))[c]
                place_ghost(
                    k, tile, c, xg.at[c, tile, k],
                    col[c, k, tile, every(near, stride=16), :], col[c, k, tile, every(far, stride=16), :],
                )
        return carry

    lax.fori_loop(0, 2, gather_x, 0)

    @pl.when(side == 1)
    def _():
        for w in range(2):
            high_corner[w].wait_recv()
            low_corner[w].wait_recv()
            relay_c[w].start()

    @pl.when(side == 0)
    def _():
        for copy in relay_c:
            copy.wait_recv()

    lane8 = lanes_of((8, 128))
    for k in range(2):
        for c in range(2):
            for g in range(3):
                up = pltpu.roll(cp[0, c, k], (96 - 32 * g) % 128, 1)
                down = cp[1, c, k]
                down = pltpu.roll(down, (-32 * g) % 128, 1) if g else down
                ux[k, c, 8 * g : 8 * g + 8, :] = jnp.where(lane8 < 64, down, up)
            near, far = ((7, 6), (24, 25))[c]
            place_ghost(k, 2, c, ux.at[k, c], ext[k, 2, every(near), :], ext[k, 2, every(far), :])

    @pl.when(side == 1)
    def _():
        for copy in high_corner + face[1] + [high, relay_x] + relay_y + relay_c:
            copy.wait_send()

    @pl.when(side == 0)
    def _():
        for copy in low_corner + face[0] + [low]:
            copy.wait_send()

    raw.wait_send()


def stream(source, q, row, tiles):
    _, step_y, step_z = VELOCITIES[q]
    need = sorted({(t - d) % 3 for t in tiles for d in ((0, step_y) if step_y else (0,))})
    data = [{t: source[k, t, pl.ds(row, 8), :] for t in need} for k in range(2)]
    lane = lanes_of((8, 128))

    def turn(value, shift):
        return pltpu.roll(value, shift % 128, 1) if shift % 128 else value

    if step_z:
        at_edge = lane % 16 == (0 if step_z == 1 else 15)
        moved = [
            {
                t: jnp.where(
                    at_edge,
                    turn(data[1 - k][t], 16 * step_y - 15 * step_z),
                    turn(data[k][t], 16 * step_y + step_z),
                )
                for t in need
            }
            for k in range(2)
        ]
    else:
        moved = [{t: turn(data[k][t], 16 * step_y) for t in need} for k in range(2)]
    if step_y:
        crossed = lane < 16 if step_y == 1 else lane >= 112
        moved = [
            {t: jnp.where(crossed, moved[k][(t - step_y) % 3], moved[k][t]) for t in tiles}
            for k in range(2)
        ]
    return moved


def advance(ext, tab, out, nxt, fs):
    me_x = lax.axis_index("bx")
    side = lax.rem(me_x, 2)
    mate = me_x + 1 - 2 * side

    def bit(table, device, k):
        row = tab[table]
        hit = (lanes_of(row.shape) == device) & (lax.broadcasted_iota(jnp.int32, row.shape, 0) == k)
        return jnp.sum(jnp.where(hit, row, 0).astype(F32))

    own_live = [bit(0, me_x, k) for k in range(2)]
    own_moving = [bit(1, me_x, k) for k in range(2)]
    arriving = [bit(1, mate, k) for k in range(2)]
    swap = (own_live[0] + own_live[1] < 0.5) & (arriving[0] + arriving[1] > 0.5)
    chosen = [
        jnp.where(swap, arriving[k], own_live[k] * (1.0 - own_moving[k])) > 0.5 for k in range(2)
    ]

    def arrive(source, stride, base, q, row, tiles):
        moved = stream(source, q, q * stride + base + row - VELOCITIES[q][0], tiles)
        result = {}
        for k in range(2):
            for t in tiles:
                value = moved[k][t]
                if q:
                    back = source[k, t, pl.ds(OPPOSITE[q] * stride + base + row, 8), :]
                    value = jnp.where(value > SOLID_TEST, value, back)
                result[k, t] = value
        return result

    for chunk in range(3):
        for q in range(19):
            for (k, t), value in arrive(ext, 32, 7, q, 8 * chunk, (0, 1, 2)).items():
                fs[q, k, t] = value
        for k in range(2):
            for t in range(3):
                f = [fs[q, k, t] for q in range(19)]
                fluid = f[0] > SOLID_TEST
                for q, value in enumerate(collide(f)):
                    nxt[k, t, q * 24 + 8 * chunk : q * 24 + 8 * chunk + 8, :] = jnp.where(
                        fluid, value, SOLID
                    )

    zero = jnp.zeros((8, 128), F32)
    both = chosen[0] & chosen[1]
    for chunk in range(2):
        for q in range(19):
            values = arrive(nxt, 24, 1, q, 8 * chunk, (0, 1))
            for t in range(2):
                spot = (q, slice(8 * chunk, 8 * chunk + 8), slice(128 * t, 128 * t + 128))
                lower, upper = values[0, t], values[1, t]
                out[(0,) + spot] = jnp.where(chosen[0], lower, jnp.where(chosen[1], upper, zero))
                out[(1,) + spot] = jnp.where(both, upper, zero)


VMEM = pl.BlockSpec(memory_space=pltpu.VMEM)
HBM = pl.BlockSpec(memory_space=pltpu.HBM)


def shards(n_x, n_y, populations, live_blocks, moving):
    pop, live, move = (
        pltpu.with_memory_space_constraint(array, pltpu.HBM)
        for array in (
            populations.reshape(2, 19, 16, 256),
            jnp.transpose(live_blocks, (1, 2, 0)),
            jnp.transpose(moving, (1, 2, 0)),
        )
    )
    parts = pl.pallas_call(
        functools.partial(exchange, n_x, n_y),
        out_shape=[
            jax.ShapeDtypeStruct((2, 3, 19 * 32, 128), F32),
            jax.ShapeDtypeStruct((2, 2, n_x), jnp.int32),
        ],
        in_specs=[HBM] * 3,
        out_specs=[VMEM] * 2,
        scratch_shapes=[
            pltpu.VMEM((2, 2, 2, 304, 128), F32),
            pltpu.VMEM((2, 2, 2, 24, 128), F32),
            pltpu.VMEM((2, 2, 2, 3, 16, 128), F32),
            pltpu.VMEM((2, 2, 2, 8, 128), F32),
            pltpu.VMEM((2, 2, 19, 16, 256), F32),
            pltpu.VMEM((2, 2, 2, 24, 128), F32),
            pltpu.VMEM((2, 2, 2, 3, 16, 128), F32),
            pltpu.VMEM((2, 2, 2, 8, 128), F32),
            pltpu.VMEM((2, 2, 24, 128), F32),
            pltpu.SemaphoreType.DMA((3,)),
            pltpu.SemaphoreType.DMA((16,)),
            pltpu.SemaphoreType.DMA((16,)),
            pltpu.SemaphoreType.REGULAR,
        ],
        compiler_params=pltpu.CompilerParams(
            collective_id=0, has_side_effects=True, vmem_limit_bytes=12 << 20
        ),
        name="exchange",
    )(pop, live, move)
    result = pl.pallas_call(
        advance,
        out_shape=jax.ShapeDtypeStruct((2, 19, 16, 256), F32),
        in_specs=[VMEM] * 2,
        out_specs=VMEM,
        scratch_shapes=[
            pltpu.VMEM((2, 3, 19 * 24, 128), F32),
            pltpu.VMEM((19, 2, 3, 8, 128), F32),
        ],
        compiler_params=pltpu.CompilerParams(vmem_limit_bytes=12 << 20),
        name="advance",
    )(*parts)
    return result.reshape(1, 1, 2, 19, 16, 256)


def solution(mesh):
    n_x, n_y = mesh.shape["bx"], mesh.shape["by"]
    placed = (P("bx", "by", None, None, None, None), P(), P())
    return jax.shard_map(
        functools.partial(shards, n_x, n_y),
        mesh=mesh,
        in_specs=placed,
        out_specs=P("bx", "by", None, None, None, None),
        check_vma=False,
    )
```
